256 devices in a mesh: tm: 16 (over z, core), height: 4 (over x), chan: 4 (over y).
Axes of the slice: x: 4, y: 4, z: 8, core: 2. Of those that a mesh axis runs over, the one named last changes fastest.
Arguments:
- frames: bfloat16 [32, 16, 256, 128], P('tm', 'height', 'chan'), may hold values from -6 to 6
- grad_out: bfloat16 [32, 16, 256, 128], P('tm', 'height', 'chan'), may hold values from -6 to 6
- weight_one: bfloat16 [256, 3, 3, 3, 256], P('chan'), may hold values from -0.078125 to 0.078125
- weight_two: bfloat16 [256, 3, 3, 3, 256], P('chan'), may hold values from -0.078125 to 0.078125
Outputs:
- grad_frames: bfloat16 [32, 16, 256, 128], P('tm', 'height', 'chan')
- grad_one: float32 [256, 3, 3, 3, 256], P('chan')
- grad_two: float32 [256, 3, 3, 3, 256], P('chan')
The draws below stay inside these ranges and needn't reach their ends.
All inputs are finite; a program needn't handle non-finite values.
Results may differ from the reference program's by a relative error of at most 0.015.
Values may be sent and summed in bfloat16 or wider, within the bound.
No kernel may reach another device: no remote copies, remote signals or barrier semaphores. Data moves between devices by JAX's collectives and lax.ppermute only.
A program may use at most 128 MiB of HBM per device.

```python
import jax
import jax.numpy as jnp
from jax import lax

CHANNELS = 256
COLS = 128
FRAMES = 32
HEIGHT_ROWS = 16


def levels(rng, shape, cuts, smallest, top_value):
    loudness, own = 1.0, jax.random.fold_in(rng, 6)
    for axis_at, shards_of in cuts:
        draws = jnp.exp(jax.random.uniform(jax.random.fold_in(own, axis_at), (shards_of,), jnp.float32, smallest / len(cuts), top_value / len(cuts)))
        loudness = loudness * jnp.repeat(draws, shape[axis_at] // shards_of).reshape([-1 if axis == axis_at else 1 for axis in range(len(shape))])
    return loudness


def scatter_about(stream_key, extent, scale, bound, cuts=(), held_as=jnp.bfloat16):
    level = levels(stream_key, extent, cuts, -0.22, 0.18) if cuts else 1.0
    entries = jax.random.normal(stream_key, extent, jnp.float32) * scale * level
    return jnp.minimum(jnp.maximum(entries, -bound), bound).astype(held_as)


def setup_inputs(seed: int = 0) -> dict:
    streams_of = jax.random.split(jax.random.key(seed), 5)
    return {
        "frames": scatter_about(streams_of[0], (FRAMES, HEIGHT_ROWS, CHANNELS, COLS), 1.0, 6.0, ((0, 16), (1, 4), (2, 4))),
        "grad_out": scatter_about(streams_of[1], (FRAMES, HEIGHT_ROWS, CHANNELS, COLS), 1.0, 6.0, ((0, 16), (1, 4), (2, 4))),
        "weight_one": scatter_about(streams_of[2], (CHANNELS, 3, 3, 3, CHANNELS), (27 * CHANNELS) ** -0.5, 0.078125, ((0, 4),)),
        "weight_two": scatter_about(streams_of[3], (CHANNELS, 3, 3, 3, CHANNELS), (27 * CHANNELS) ** -0.5, 0.078125, ((0, 4),)),
    }


def product(form, left, right):
    return jnp.einsum(form, left.astype(jnp.float32), right.astype(jnp.float32), precision=lax.Precision.HIGHEST)


def forward_taps(padded, weight):
    frame_count = padded.shape[0] - 2
    row_count = padded.shape[1] - 2
    col_count = padded.shape[3] - 2
    summed = jnp.zeros((frame_count, row_count, weight.shape[0], col_count), jnp.float32)
    for time_tap in range(3):
        for row_tap in range(3):
            for col_tap in range(3):
                window = padded[time_tap:time_tap + frame_count, row_tap:row_tap + row_count, :, col_tap:col_tap + col_count]
                summed = summed + product("frcw,oc->frow", window, weight[:, time_tap, row_tap, col_tap, :])
    return summed


def backward_taps(padded, weight):
    frame_count = padded.shape[0] - 2
    row_count = padded.shape[1] - 2
    col_count = padded.shape[3] - 2
    summed = jnp.zeros((frame_count, row_count, weight.shape[4], col_count), jnp.float32)
    for time_tap in range(3):
        for row_tap in range(3):
            for col_tap in range(3):
                window = padded[2 - time_tap:2 - time_tap + frame_count, 2 - row_tap:2 - row_tap + row_count, :, 2 - col_tap:2 - col_tap + col_count]
                summed = summed + product("frow,oc->frcw", window, weight[:, time_tap, row_tap, col_tap, :])
    return summed


def forward_filter(padded, gradient):
    frame_count, row_count, out_width, col_count = gradient.shape
    pieces = []
    for time_tap in range(3):
        for row_tap in range(3):
            for col_tap in range(3):
                window = padded[time_tap:time_tap + frame_count, row_tap:row_tap + row_count, :, col_tap:col_tap + col_count]
                pieces.append(product("frcw,frow->oc", window, gradient))
    return jnp.stack(pieces, 1).reshape(out_width, 3, 3, 3, padded.shape[2])


def backward_filter(source, padded):
    frame_count, row_count, in_width, col_count = source.shape
    pieces = []
    for time_tap in range(3):
        for row_tap in range(3):
            for col_tap in range(3):
                window = padded[2 - time_tap:2 - time_tap + frame_count, 2 - row_tap:2 - row_tap + row_count, :, 2 - col_tap:2 - col_tap + col_count]
                pieces.append(product("frcw,frow->oc", source, window))
    return jnp.stack(pieces, 1).reshape(padded.shape[2], 3, 3, 3, in_width)


def reference(frames, grad_out, weight_one, weight_two):
    frames_padded = jnp.pad(frames, ((2, 0), (1, 1), (0, 0), (1, 1)))
    pre = forward_taps(frames_padded, weight_one)
    act = jax.nn.silu(pre).astype(jnp.bfloat16)
    grads_padded = jnp.pad(grad_out, ((0, 2), (1, 1), (0, 0), (1, 1)))
    grad_act = backward_taps(grads_padded, weight_two)
    sigmoid_pre = jax.nn.sigmoid(pre)
    grad_pre = (grad_act * sigmoid_pre * (1.0 + pre * (1.0 - sigmoid_pre))).astype(jnp.bfloat16)
    pre_padded = jnp.pad(grad_pre, ((0, 2), (1, 1), (0, 0), (1, 1)))
    grad_frames = backward_taps(pre_padded, weight_one).astype(jnp.bfloat16)
    grad_one = forward_filter(frames_padded, grad_pre)
    grad_two = backward_filter(act, grads_padded)
    return (grad_frames, grad_one, grad_two)
```

```python
import jax
import jax.numpy as jnp
from jax import lax
from jax.sharding import PartitionSpec as P


def passed_along(block, axis, distance):
    devices = range(lax.axis_size(axis))
    route = [(i - distance, i) for i in devices if i - distance in devices]
    return lax.ppermute(block, axis, route)


def extended(cells, sides, width):
    for axis, dim in sides:
        count = lax.axis_size(axis)
        ends = count - 1
        head = lax.slice_in_dim(cells, 0, width, axis=dim)
        tail = lax.slice_in_dim(cells, cells.shape[dim] - width, cells.shape[dim], axis=dim)
        cells = jnp.concatenate(
            [
                lax.ppermute(tail, axis, [(i, (i + 1) % count) for i in range(ends)]),
                cells,
                lax.ppermute(head, axis, [((i + 1) % count, i) for i in range(ends)]),
            ],
            axis=dim,
        )
    return cells


def product(form, left, right):
    return jnp.einsum(form, left, right, preferred_element_type=jnp.float32)


def shift_cols(block, offset):
    if offset == 0:
        return block
    edge = jnp.zeros(block.shape[:3] + (1,), block.dtype)
    if offset > 0:
        return jnp.concatenate([block[..., 1:], edge], 3)
    return jnp.concatenate([edge, block[..., :-1]], 3)


def forward_taps(padded, weight):
    frame_count = padded.shape[0] - 2
    row_count = padded.shape[1] - 2
    col_count = padded.shape[3]
    summed = jnp.zeros((frame_count, row_count, weight.shape[0], col_count), jnp.float32)
    for col_tap in range(3):
        partial_sum = jnp.zeros((frame_count, row_count, weight.shape[0], col_count), jnp.float32)
        for time_tap in range(3):
            for row_tap in range(3):
                window = padded[time_tap : time_tap + frame_count, row_tap : row_tap + row_count]
                partial_sum = partial_sum + product(
                    "frcw,oc->frow", window, weight[:, time_tap, row_tap, col_tap, :]
                )
        summed = summed + shift_cols(partial_sum, col_tap - 1)
    return summed


def backward_taps(padded, weight):
    frame_count = padded.shape[0] - 2
    row_count = padded.shape[1] - 2
    col_count = padded.shape[3]
    summed = jnp.zeros((frame_count, row_count, weight.shape[4], col_count), jnp.float32)
    for col_tap in range(3):
        partial_sum = jnp.zeros((frame_count, row_count, weight.shape[4], col_count), jnp.float32)
        for time_tap in range(3):
            for row_tap in range(3):
                window = padded[
                    2 - time_tap : 2 - time_tap + frame_count, 2 - row_tap : 2 - row_tap + row_count
                ]
                partial_sum = partial_sum + product(
                    "frow,oc->frcw", window, weight[:, time_tap, row_tap, col_tap, :]
                )
        summed = summed + shift_cols(partial_sum, 1 - col_tap)
    return summed


def forward_filter(padded, gradient):
    frame_count, row_count, out_width, col_count = gradient.shape
    moved = [shift_cols(gradient, 1 - col_tap) for col_tap in range(3)]
    pieces = []
    for time_tap in range(3):
        for row_tap in range(3):
            window = padded[time_tap : time_tap + frame_count, row_tap : row_tap + row_count]
            for col_tap in range(3):
                pieces.append(product("frcw,frow->oc", window, moved[col_tap]))
    return jnp.stack(pieces, 1).reshape(out_width, 3, 3, 3, padded.shape[2])


def backward_filter(source, padded):
    frame_count, row_count, in_width, col_count = source.shape
    moved = [shift_cols(padded, 1 - col_tap) for col_tap in range(3)]
    pieces = []
    for time_tap in range(3):
        for row_tap in range(3):
            for col_tap in range(3):
                window = moved[col_tap][
                    2 - time_tap : 2 - time_tap + frame_count, 2 - row_tap : 2 - row_tap + row_count
                ]
                pieces.append(product("frcw,frow->oc", source, window))
    return jnp.stack(pieces, 1).reshape(padded.shape[2], 3, 3, 3, in_width)


def rotated(block, axis, distance):
    count = lax.axis_size(axis)
    return lax.ppermute(block, axis, [(i, (i + distance) % count) for i in range(count)])


def in_order(own, others, axis):
    me = lax.axis_index(axis)
    count = len(others) + 1
    pieces = [others[count - 2 - i] for i in range(count - 1)] + [own]
    ring = jnp.stack(pieces + pieces[:-1], 0)
    return lax.dynamic_slice_in_dim(ring, (count - 1 - me) % count, count, 0)


def gathered(block, axis):
    return in_order(block, [rotated(block, axis, k) for k in range(1, lax.axis_size(axis))], axis)


def scattered(parts, axis):
    me = lax.axis_index(axis)
    count = parts.shape[0]
    pick = lambda k: lax.dynamic_index_in_dim(parts, (me + k) % count, 0, keepdims=False)
    total = pick(0)
    for k in range(1, count):
        total = total + rotated(pick(k).astype(jnp.bfloat16), axis, k).astype(jnp.float32)
    return total


def swapped(block, distance):
    return lax.ppermute(block, "tm", [(i, i ^ distance) for i in range(lax.axis_size("tm"))])


def halves_summed(block, bit, distance):
    half = block.shape[0] // 2
    low, high = block[:half], block[half:]
    mine = jnp.where(bit == 1, high, low)
    theirs = jnp.where(bit == 1, low, high)
    return mine + swapped(theirs.astype(jnp.bfloat16), distance).astype(jnp.float32)


def halves_joined(block, bit, distance):
    other = swapped(block, distance)
    return jnp.concatenate([jnp.where(bit == 1, other, block), jnp.where(bit == 1, block, other)], 0)


def summed_filters(part_one, part_two):
    place = lax.axis_index("tm")
    core, z_one, z_two = place % 2, (place // 2) % 2, (place // 4) % 2
    parts = jnp.stack([part_one, part_two], 0).reshape(2 * 1728, 256)
    total = halves_summed(parts, core, 1)
    total = scattered(total.reshape(4, 864, 128), "height")
    total = halves_summed(total, z_one, 2)
    total = halves_summed(total, z_two, 4)
    total = total.astype(jnp.bfloat16)
    total = (total.astype(jnp.float32) + swapped(total, 8).astype(jnp.float32)).astype(jnp.bfloat16)
    total = halves_joined(total, z_two, 4)
    total = halves_joined(total, z_one, 2)
    total = gathered(total, "height").reshape(1728, 256)
    total = halves_joined(total, core, 1).reshape(2, 64, 3, 3, 3, 256).astype(jnp.float32)
    return total[0], total[1]


def joined_channels(block):
    panel = jnp.moveaxis(gathered(block, "chan"), 0, 2)
    return panel.reshape(block.shape[:2] + (256,) + block.shape[3:])


def split_channels(block):
    return jnp.moveaxis(block.reshape(block.shape[:2] + (4, 64) + block.shape[3:]), 2, 0)


def on_device(frames, grad_out, weight_one, weight_two):
    frames_full = joined_channels(frames)
    earlier = passed_along(frames_full, "tm", 1)
    frames_time = jnp.concatenate([earlier, frames_full], 0)
    frames_panel = extended(frames_time, (("height", 1),), 1)
    pre = forward_taps(frames_panel, weight_one)
    act = jax.nn.silu(pre).astype(jnp.bfloat16)
    later = passed_along(grad_out, "tm", -1)
    grads_time = jnp.concatenate([grad_out, later], 0)
    grads_padded = extended(grads_time, (("height", 1),), 1)
    act_full = joined_channels(act)
    part_two = backward_filter(act_full, grads_padded)
    sigmoid_pre = jax.nn.sigmoid(pre)
    grad_act = scattered(split_channels(backward_taps(grads_padded, weight_two)), "chan")
    grad_pre = (grad_act * sigmoid_pre * (1.0 + pre * (1.0 - sigmoid_pre))).astype(jnp.bfloat16)
    pre_later = passed_along(grad_pre, "tm", -1)
    pre_time = jnp.concatenate([grad_pre, pre_later], 0)
    pre_padded = extended(pre_time, (("height", 1),), 1)
    grad_frames = scattered(split_channels(backward_taps(pre_padded, weight_one)), "chan")
    part_one = forward_filter(frames_panel, grad_pre)
    grad_one, grad_two = summed_filters(part_one, part_two)
    return (grad_frames.astype(jnp.bfloat16), grad_one, grad_two)


def solution(mesh):
    in_specs = (
        P("tm", "height", "chan", None),
        P("tm", "height", "chan", None),
        P("chan", None, None, None, None),
        P("chan", None, None, None, None),
    )
    out_specs = (
        P("tm", "height", "chan", None),
        P("chan", None, None, None, None),
        P("chan", None, None, None, None),
    )
    return jax.shard_map(
        on_device, mesh=mesh, in_specs=in_specs, out_specs=out_specs, check_vma=False
    )
```

```python
import jax
import jax.numpy as jnp
from jax import lax
from jax.experimental import pallas as pl
from jax.experimental.pallas import tpu as pltpu
from jax.sharding import PartitionSpec as P


def passed_along(block, axis, distance):
    devices = range(lax.axis_size(axis))
    route = [(i - distance, i) for i in devices if i - distance in devices]
    return lax.ppermute(block, axis, route)


VMEM_LIMIT = 50 * 1024 * 1024
TAPS = [(a, b) for a in range(3) for b in range(3)]
SPOTS = [(t, i) for t in range(2) for i in range(4)]


def call(body, outs, scratch, place, *operands):
    vmem = pl.BlockSpec(memory_space=pltpu.VMEM)
    return pl.pallas_call(
        body,
        out_shape=outs,
        in_specs=[pl.BlockSpec(memory_space=pltpu.SMEM)] + [vmem] * len(operands),
        out_specs=[vmem] * len(outs),
        scratch_shapes=scratch,
        compiler_params=pltpu.CompilerParams(vmem_limit_bytes=VMEM_LIMIT),
    )(place, *operands)


def lanes_moved(cell):
    wide = cell.astype(jnp.float32)
    lane = lax.broadcasted_iota(jnp.int32, wide.shape, 1)
    ahead = jnp.where(lane == 127, 0.0, pltpu.roll(wide, 127, 1))
    behind = jnp.where(lane == 0, 0.0, pltpu.roll(wide, 1, 1))
    return ahead.astype(jnp.bfloat16), cell, behind.astype(jnp.bfloat16)


def forward_body(place, own, early, above, below, weight, panel, pre, act, wide):
    me = place[0]
    for f in range(4):
        for r in range(6):
            if r == 0:
                cell = above[f, 0]
            elif r == 5:
                cell = below[f, 0]
            else:
                cell = early[f, r - 1] if f < 2 else own[f - 2, r - 1]
            for k in range(4):
                at = pl.multiple_of(((me + 4 - k) % 4) * 64, 64)
                panel[f * 6 + r, pl.ds(at, 64), :] = cell[k * 64 : k * 64 + 64]
    for p, (t, i) in enumerate(SPOTS):
        for n, (a, b) in enumerate(TAPS):
            wide[n * 256 : n * 256 + 256, p * 128 : p * 128 + 128] = panel[(t + a) * 6 + i + b]
    for t in range(2):
        sums = jnp.dot(
            weight[...], wide[:, t * 512 : t * 512 + 512], preferred_element_type=jnp.float32
        )
        lane = lax.broadcasted_iota(jnp.int32, (64, 128), 1)
        for i in range(4):
            part = sums[:, i * 128 : i * 128 + 128]
            behind = jnp.where(lane == 0, 0.0, pltpu.roll(part[:64], 1, 1))
            ahead = jnp.where(lane == 127, 0.0, pltpu.roll(part[128:], 127, 1))
            value = behind + part[64:128] + ahead
            pre[t * 4 + i] = value
            act[t * 4 + i] = (value * jax.nn.sigmoid(value)).astype(jnp.bfloat16)


def spread(own, late, above, below, wide):
    for f in range(4):
        for r in range(6):
            if r == 0:
                cell = above[f, 0]
            elif r == 5:
                cell = below[f, 0]
            else:
                cell = own[f, r - 1] if f < 2 else late[f - 2, r - 1]
            moved = lanes_moved(cell)
            for n, (a, b) in enumerate(TAPS):
                t, i = f - 2 + a, r - 2 + b
                if (t, i) in SPOTS:
                    p = SPOTS.index((t, i))
                    for e in range(3):
                        row = (n * 3 + e) * 64
                        wide[row : row + 64, p * 128 : p * 128 + 128] = moved[e]


def transposed_body(place, own, late, above, below, weight, mine, one, two, three, wide, full):
    me = place[0]
    spread(own, late, above, below, wide)
    full[...] = jnp.dot(weight[...], wide[...], preferred_element_type=jnp.float32)
    for k, out in enumerate((mine, one, two, three)):
        at = pl.multiple_of(((me + k) % 4) * 64, 64)
        for p in range(8):
            out[p] = full[pl.ds(at, 64), p * 128 : p * 128 + 128].astype(out.dtype)


def against(left, right):
    return lax.dot_general(left, right, (((1,), (1,)), ((), ())), preferred_element_type=jnp.float32)


def store_filter(out, height, tap, rows):
    for q in range(4):
        out[(q + 4 - height) % 4, tap] = rows[q * 16 : q * 16 + 16].astype(jnp.bfloat16)


def first_filter_body(place, panel, gradient, out, moved):
    height = place[1]
    for p in range(8):
        for e, part in enumerate(lanes_moved(gradient[p])):
            moved[e * 64 : e * 64 + 64, p * 128 : p * 128 + 128] = part
    for n, (a, b) in enumerate(TAPS):
        window = jnp.concatenate([panel[(t + a) * 6 + i + b] for t, i in SPOTS], 1)
        sums = against(moved[...], window)
        for e in range(3):
            store_filter(out, height, n * 3 + e, sums[e * 64 : e * 64 + 64])


def second_filter_body(place, own, late, above, below, a0, a1, a2, a3, out, wide, acts):
    me, height = place[0], place[1]
    spread(own, late, above, below, wide)
    for k, part in enumerate((a0, a1, a2, a3)):
        at = pl.multiple_of(((me + 4 - k) % 4) * 64, 64)
        for p in range(8):
            acts[pl.ds(at, 64), p * 128 : p * 128 + 128] = part[p]
    for n in range(9):
        sums = against(wide[n * 192 : n * 192 + 192], acts[...])
        for e in range(3):
            store_filter(out, height, n * 3 + e, sums[e * 64 : e * 64 + 64])


def shaped(shape, dtype):
    return jax.ShapeDtypeStruct(shape, dtype)


def forward(place, own, early, above, below, weight):
    return call(
        forward_body,
        [shaped((24, 256, 128), jnp.bfloat16), shaped((8, 64, 128), jnp.float32), shaped((8, 64, 128), jnp.bfloat16)],
        [pltpu.VMEM((2304, 1024), jnp.bfloat16)],
        place, own, early, above, below, weight,
    )


def transposed(place, cells, weight):
    return call(
        transposed_body,
        [shaped((8, 64, 128), jnp.float32)] + [shaped((8, 64, 128), jnp.bfloat16)] * 3,
        [pltpu.VMEM((1728, 1024), jnp.bfloat16), pltpu.VMEM((256, 1024), jnp.float32)],
        place, *cells, weight,
    )


def first_filter(place, panel, gradient):
    return call(
        first_filter_body, [shaped((4, 27, 16, 256), jnp.bfloat16)],
        [pltpu.VMEM((192, 1024), jnp.bfloat16)], place, panel, gradient,
    )[0]


def second_filter(place, cells, acts):
    return call(
        second_filter_body, [shaped((4, 27, 16, 256), jnp.bfloat16)],
        [pltpu.VMEM((1728, 1024), jnp.bfloat16), pltpu.VMEM((256, 1024), jnp.bfloat16)],
        place, *cells, *acts,
    )[0]


def rotated(block, axis, distance):
    count = lax.axis_size(axis)
    return lax.ppermute(block, axis, [(i, (i + distance) % count) for i in range(count)])


def in_order(own, others, axis):
    me = lax.axis_index(axis)
    count = len(others) + 1
    pieces = [others[count - 2 - i] for i in range(count - 1)] + [own]
    ring = jnp.stack(pieces + pieces[:-1], 0)
    return lax.dynamic_slice_in_dim(ring, (count - 1 - me) % count, count, 0)


def all_rotated(block, axis):
    return [rotated(block, axis, k) for k in range(1, lax.axis_size(axis))]


def exchanged(pieces, axis):
    total = pieces[0].astype(jnp.float32)
    for k in range(1, len(pieces)):
        total = total + rotated(pieces[k], axis, k).astype(jnp.float32)
    return total


def swapped(block, distance):
    return lax.ppermute(block, "tm", [(i, i ^ distance) for i in range(lax.axis_size("tm"))])


def sum_of_halves(low, high, bit, distance):
    mine = jnp.where(bit == 1, high, low)
    theirs = jnp.where(bit == 1, low, high)
    other = swapped(theirs.astype(jnp.bfloat16), distance)
    return mine.astype(jnp.float32) + other.astype(jnp.float32)


def halves_joined(block, bit, distance, dim=0):
    other = swapped(block, distance)
    return jnp.concatenate([jnp.where(bit == 1, other, block), jnp.where(bit == 1, block, other)], dim)


def summed_filters(part_one, part_two):
    spot = lax.axis_index("tm")
    core, z_one, z_two = spot % 2, (spot // 2) % 2, (spot // 4) % 2
    total = sum_of_halves(part_one, part_two, core, 1)
    total = exchanged([total[0]] + [total[k].astype(jnp.bfloat16) for k in range(1, 4)], "height")
    total = sum_of_halves(total[:, :8], total[:, 8:], z_one, 2)
    total = sum_of_halves(total[..., :128], total[..., 128:], z_two, 4)
    total = total.astype(jnp.bfloat16)
    total = (total.astype(jnp.float32) + swapped(total, 8).astype(jnp.float32)).astype(jnp.bfloat16)
    total = halves_joined(total, z_two, 4, 2)
    total = halves_joined(total.transpose(1, 0, 2).reshape(432, 128), z_one, 2)
    total = in_order(total, all_rotated(total, "height"), "height").reshape(1728, 256)
    total = halves_joined(total, core, 1).reshape(2, 64, 3, 3, 3, 256).astype(jnp.float32)
    return total[0], total[1]


def edges(first, second):
    last = first.shape[1] - 1
    heads = jnp.concatenate([first[:, :1], second[:, :1]], 0)
    tails = jnp.concatenate([first[:, last:], second[:, last:]], 0)
    return passed_along(tails, "height", 1), passed_along(heads, "height", -1)


def with_later(cells):
    late = passed_along(cells, "tm", -1)
    return (cells, late) + edges(cells, late)


def on_device(frames, grad_out, weight_one, weight_two):
    place = jnp.stack([lax.axis_index("chan"), lax.axis_index("height")]).astype(jnp.int32)
    frames_all = jnp.concatenate([frames] + all_rotated(frames, "chan"), 2)
    early = passed_along(frames_all, "tm", 1)
    above, below = edges(early, frames_all)
    ahead = weight_one.transpose(3, 0, 1, 2, 4).reshape(192, 2304)
    back_one = weight_one.transpose(4, 1, 2, 3, 0).reshape(256, 1728)
    back_two = weight_two.transpose(4, 1, 2, 3, 0).reshape(256, 1728)
    panel, pre, act = forward(place, frames_all, early, above, below, ahead)
    grads = with_later(grad_out)
    grad_act = exchanged(transposed(place, grads, back_two), "chan")
    sigmoid_pre = jax.nn.sigmoid(pre)
    grad_pre = (grad_act * sigmoid_pre * (1.0 + pre * (1.0 - sigmoid_pre))).astype(jnp.bfloat16)
    part_one = first_filter(place, panel, grad_pre)
    part_two = second_filter(place, grads, [act] + all_rotated(act, "chan"))
    grad_one, grad_two = summed_filters(part_one, part_two)
    cells = with_later(grad_pre.reshape(2, 4, 64, 128))
    grad_frames = exchanged(transposed(place, cells, back_one), "chan")
    return (grad_frames.reshape(2, 4, 64, 128).astype(jnp.bfloat16), grad_one, grad_two)


def solution(mesh):
    in_specs = (
        P("tm", "height", "chan", None),
        P("tm", "height", "chan", None),
        P("chan", None, None, None, None),
        P("chan", None, None, None, None),
    )
    out_specs = (
        P("tm", "height", "chan", None),
        P("chan", None, None, None, None),
        P("chan", None, None, None, None),
    )
    return jax.shard_map(
        on_device, mesh=mesh, in_specs=in_specs, out_specs=out_specs, check_vma=False
    )
```

```python
import jax
import jax.numpy as jnp
from jax import lax
from jax.experimental import pallas as pl
from jax.experimental.pallas import tpu as pltpu
from jax.sharding import PartitionSpec as P


def passed_along(block, axis, distance):
    devices = range(lax.axis_size(axis))
    route = [(i - distance, i) for i in devices if i - distance in devices]
    return lax.ppermute(block, axis, route)


VMEM_LIMIT = 50 * 1024 * 1024
TAPS = [(a, b) for a in range(3) for b in range(3)]
SPOTS = [(t, i) for t in range(2) for i in range(4)]


def call(body, outs, scratch, place, *operands, after=()):
    vmem = pl.BlockSpec(memory_space=pltpu.VMEM)
    used = 1 + len(operands)
    rest = used + len(after)
    return pl.pallas_call(
        lambda *refs: body(*refs[:used], *refs[rest:]),
        out_shape=outs,
        in_specs=[pl.BlockSpec(memory_space=pltpu.SMEM)]
        + [vmem] * len(operands)
        + [pl.BlockSpec(memory_space=pl.ANY)] * len(after),
        out_specs=[vmem] * len(outs),
        scratch_shapes=scratch,
        compiler_params=pltpu.CompilerParams(vmem_limit_bytes=VMEM_LIMIT),
    )(place, *operands, *after)


def lanes_moved(cell):
    wide = cell.astype(jnp.float32)
    lane = lax.broadcasted_iota(jnp.int32, wide.shape, 1)
    ahead = jnp.where(lane == 127, 0.0, pltpu.roll(wide, 127, 1))
    behind = jnp.where(lane == 0, 0.0, pltpu.roll(wide, 1, 1))
    return ahead.astype(jnp.bfloat16), cell, behind.astype(jnp.bfloat16)


def forward_body(place, own, early, above, below, weight, panel, pre, act, wide, flat):
    me = place[0]
    for n in range(9):
        flat[:, n * 256 : n * 256 + 256] = weight[n]
    for f in range(4):
        for r in range(6):
            if r == 0:
                cell = above[f, 0]
            elif r == 5:
                cell = below[f, 0]
            else:
                cell = early[f, r - 1] if f < 2 else own[f - 2, r - 1]
            for k in range(4):
                at = pl.multiple_of(((me + 4 - k) % 4) * 64, 64)
                panel[f * 6 + r, pl.ds(at, 64), :] = cell[k * 64 : k * 64 + 64]
    for p, (t, i) in enumerate(SPOTS):
        for n, (a, b) in enumerate(TAPS):
            wide[n * 256 : n * 256 + 256, p * 128 : p * 128 + 128] = panel[(t + a) * 6 + i + b]
    for t in range(2):
        sums = jnp.dot(
            flat[...], wide[:, t * 512 : t * 512 + 512], preferred_element_type=jnp.float32
        )
        lane = lax.broadcasted_iota(jnp.int32, (64, 128), 1)
        for i in range(4):
            part = sums[:, i * 128 : i * 128 + 128]
            behind = jnp.where(lane == 0, 0.0, pltpu.roll(part[:64], 1, 1))
            ahead = jnp.where(lane == 127, 0.0, pltpu.roll(part[128:], 127, 1))
            value = behind + part[64:128] + ahead
            pre[t * 4 + i] = value
            act[t * 4 + i] = (value * jax.nn.sigmoid(value)).astype(jnp.bfloat16)


def spread(own, late, above, below, wide):
    for f in range(4):
        for r in range(6):
            if r == 0:
                cell = above[f, 0]
            elif r == 5:
                cell = below[f, 0]
            else:
                cell = own[f, r - 1] if f < 2 else late[f - 2, r - 1]
            moved = lanes_moved(cell)
            for n, (a, b) in enumerate(TAPS):
                t, i = f - 2 + a, r - 2 + b
                if (t, i) in SPOTS:
                    p = SPOTS.index((t, i))
                    for e in range(3):
                        row = (n * 3 + e) * 64
                        wide[row : row + 64, p * 128 : p * 128 + 128] = moved[e]


def transposed_body(place, own, late, above, below, weight, mine, one, two, three, wide, full):
    me = place[0]
    spread(own, late, above, below, wide)
    full[...] = lax.dot_general(
        weight[...], wide[...], (((0,), (0,)), ((), ())), preferred_element_type=jnp.float32
    )
    for k, out in enumerate((mine, one, two, three)):
        at = pl.multiple_of(((me + k) % 4) * 64, 64)
        for p in range(8):
            out[p] = full[pl.ds(at, 64), p * 128 : p * 128 + 128].astype(out.dtype)


def against(left, right):
    return lax.dot_general(left, right, (((1,), (1,)), ((), ())), preferred_element_type=jnp.float32)


def store_filter(out, height, tap, rows):
    for q in range(4):
        out[(q + 4 - height) % 4, tap] = rows[q * 16 : q * 16 + 16].astype(jnp.bfloat16)


def first_filter_body(place, panel, gradient, out, moved):
    height = place[1]
    for p in range(8):
        for e, part in enumerate(lanes_moved(gradient[p])):
            moved[e * 64 : e * 64 + 64, p * 128 : p * 128 + 128] = part
    for n, (a, b) in enumerate(TAPS):
        window = jnp.concatenate([panel[(t + a) * 6 + i + b] for t, i in SPOTS], 1)
        sums = against(moved[...], window)
        for e in range(3):
            store_filter(out, height, n * 3 + e, sums[e * 64 : e * 64 + 64])


def second_filter_body(place, own, late, above, below, a0, a1, a2, a3, out, wide, acts):
    me, height = place[0], place[1]
    spread(own, late, above, below, wide)
    for k, part in enumerate((a0, a1, a2, a3)):
        at = pl.multiple_of(((me + 4 - k) % 4) * 64, 64)
        for p in range(8):
            acts[pl.ds(at, 64), p * 128 : p * 128 + 128] = part[p]
    for n in range(9):
        sums = against(wide[n * 192 : n * 192 + 192], acts[...])
        for e in range(3):
            store_filter(out, height, n * 3 + e, sums[e * 64 : e * 64 + 64])


def shaped(shape, dtype):
    return jax.ShapeDtypeStruct(shape, dtype)


def forward(place, own, early, above, below, weight, after):
    return call(
        forward_body,
        [shaped((24, 256, 128), jnp.bfloat16), shaped((8, 64, 128), jnp.float32), shaped((8, 64, 128), jnp.bfloat16)],
        [pltpu.VMEM((2304, 1024), jnp.bfloat16), pltpu.VMEM((192, 2304), jnp.bfloat16)],
        place, own, early, above, below, weight, after=after,
    )


def transposed(place, cells, weight):
    return call(
        transposed_body,
        [shaped((8, 64, 128), jnp.float32)] + [shaped((8, 64, 128), jnp.bfloat16)] * 3,
        [pltpu.VMEM((1728, 1024), jnp.bfloat16), pltpu.VMEM((256, 1024), jnp.float32)],
        place, *cells, weight,
    )


def first_filter(place, panel, gradient):
    return call(
        first_filter_body, [shaped((4, 27, 16, 256), jnp.bfloat16)],
        [pltpu.VMEM((192, 1024), jnp.bfloat16)], place, panel, gradient,
    )[0]


def second_filter(place, cells, acts):
    return call(
        second_filter_body, [shaped((4, 27, 16, 256), jnp.bfloat16)],
        [pltpu.VMEM((1728, 1024), jnp.bfloat16), pltpu.VMEM((256, 1024), jnp.bfloat16)],
        place, *cells, *acts,
    )[0]


def quarters_body(place, own, one, two, three, mine, first, second, third, sums):
    z = place[2]
    total = own[...].astype(jnp.float32)
    for part in (one, two, three):
        total = total + part[...].astype(jnp.float32)
    for q in range(4):
        o, c = (q // 2) * 8, (q % 2) * 128
        sums[q] = total[:, o : o + 8, c : c + 128]
    for k, out in enumerate((mine, first, second, third)):
        out[...] = sums[(z + k) % 4].astype(out.dtype)


def quarters(place, pieces, after):
    small = [shaped((27, 8, 128), jnp.float32)] + [shaped((27, 8, 128), jnp.bfloat16)] * 3
    return call(
        quarters_body, small, [pltpu.VMEM((4, 27, 8, 128), jnp.float32)], place, *pieces, after=after
    )


def rejoined_body(place, own, one, two, three, out, parts):
    z = place[2]
    for k, part in enumerate((own, one, two, three)):
        parts[(z + 4 - k) % 4] = part[...]
    for q in range(4):
        o, c = (q // 2) * 8, (q % 2) * 128
        out[:, o : o + 8, c : c + 128] = parts[q]


def rejoined(place, pieces, after):
    return call(
        rejoined_body, [shaped((27, 16, 256), jnp.bfloat16)],
        [pltpu.VMEM((4, 27, 8, 128), jnp.bfloat16)], place, *pieces, after=after,
    )[0]


def stacked_body(place, own, one, two, three, out):
    height = place[1]
    for k, part in enumerate((own, one, two, three)):
        at = pl.multiple_of(((height + 4 - k) % 4) * 16, 16)
        out[:, pl.ds(at, 16), :] = part[...]


def stacked(place, pieces):
    return call(stacked_body, [shaped((27, 64, 256), jnp.bfloat16)], [], place, *pieces)[0]


def rotated(block, axis, distance):
    count = lax.axis_size(axis)
    return lax.ppermute(block, axis, [(i, (i + distance) % count) for i in range(count)])


def all_rotated(block, axis):
    return [rotated(block, axis, k) for k in range(1, lax.axis_size(axis))]


def sent_on(pieces, axis):
    return [pieces[0]] + [rotated(pieces[k], axis, k) for k in range(1, len(pieces))]


def exchanged(pieces, axis):
    return sum(part.astype(jnp.float32) for part in sent_on(pieces, axis))


def swapped(block, distance):
    return lax.ppermute(block, "tm", [(i, i ^ distance) for i in range(lax.axis_size("tm"))])


def quad_rotated(block, distance):
    route = [(i, i - i % 8 + (i + 2 * distance) % 8) for i in range(lax.axis_size("tm"))]
    return lax.ppermute(block, "tm", route)


def summed_pair(part_one, part_two, core):
    mine = jnp.where(core == 1, part_two, part_one)
    theirs = jnp.where(core == 1, part_one, part_two)
    total = mine.astype(jnp.float32) + swapped(theirs, 1).astype(jnp.float32)
    return [total[0]] + [total[k].astype(jnp.bfloat16) for k in range(1, 4)]


def rest_of_sum(place, pieces, gradient_pieces, core):
    mine, *others = quarters(place, sent_on(pieces, "height"), [gradient_pieces[0]])
    gradient = exchanged(gradient_pieces, "chan")
    total = mine
    for k, part in enumerate(others):
        total = total + quad_rotated(part, k + 1).astype(jnp.float32)
    total = total.astype(jnp.bfloat16)
    gradient = gradient.reshape(2, 4, 64, 128).astype(jnp.bfloat16)
    total = (total.astype(jnp.float32) + swapped(total, 8).astype(jnp.float32)).astype(jnp.bfloat16)
    total = rejoined(place, [total] + [quad_rotated(total, k) for k in range(1, 4)], [gradient])
    total = stacked(place, [total] + all_rotated(total, "height"))
    other = swapped(total, 1)
    one = jnp.where(core == 1, other, total).astype(jnp.float32)
    two = jnp.where(core == 1, total, other).astype(jnp.float32)
    return gradient, one, two


def filter_shape(flat):
    return flat.reshape(3, 3, 3, 64, 256).transpose(3, 0, 1, 2, 4)


def edges(first, second):
    last = first.shape[1] - 1
    heads = jnp.concatenate([first[:, :1], second[:, :1]], 0)
    tails = jnp.concatenate([first[:, last:], second[:, last:]], 0)
    return passed_along(tails, "height", 1), passed_along(heads, "height", -1)


def with_later(cells):
    late = passed_along(cells, "tm", -1)
    return (cells, late) + edges(cells, late)


def on_device(frames, grad_out, weight_one, weight_two):
    spot = lax.axis_index("tm")
    core = spot % 2
    place = jnp.stack([lax.axis_index("chan"), lax.axis_index("height"), (spot // 2) % 4]).astype(jnp.int32)
    taps_one = weight_one.transpose(1, 2, 3, 0, 4).reshape(1728, 256)
    taps_two = weight_two.transpose(1, 2, 3, 0, 4).reshape(1728, 256)
    frames_all = jnp.concatenate([frames] + all_rotated(frames, "chan"), 2)
    early = passed_along(frames_all, "tm", 1)
    above, below = edges(early, frames_all)
    grads = with_later(grad_out)
    act_pieces = transposed(place, grads, taps_two)
    panel, pre, act = forward(
        place, frames_all, early, above, below, taps_one.reshape(9, 192, 256), [act_pieces[0]]
    )
    grad_act = exchanged(act_pieces, "chan")
    sigmoid_pre = jax.nn.sigmoid(pre)
    grad_pre = (grad_act * sigmoid_pre * (1.0 + pre * (1.0 - sigmoid_pre))).astype(jnp.bfloat16)
    part_one = first_filter(place, panel, grad_pre)
    part_two = second_filter(place, grads, [act] + all_rotated(act, "chan"))
    pieces = summed_pair(part_one, part_two, core)
    cells = with_later(grad_pre.reshape(2, 4, 64, 128))
    gradient_pieces = transposed(place, cells, taps_one)
    grad_frames, grad_one, grad_two = rest_of_sum(place, pieces, gradient_pieces, core)
    return (grad_frames, filter_shape(grad_one), filter_shape(grad_two))


def solution(mesh):
    in_specs = (
        P("tm", "height", "chan", None),
        P("tm", "height", "chan", None),
        P("chan", None, None, None, None),
        P("chan", None, None, None, None),
    )
    out_specs = (
        P("tm", "height", "chan", None),
        P("chan", None, None, None, None),
        P("chan", None, None, None, None),
    )
    return jax.shard_map(
        on_device, mesh=mesh, in_specs=in_specs, out_specs=out_specs, check_vma=False
    )
```

```python
import jax
import jax.numpy as jnp
from jax import lax
from jax.experimental import pallas as pl
from jax.experimental.pallas import tpu as pltpu
from jax.sharding import PartitionSpec as P


def passed_along(block, axis, distance):
    devices = range(lax.axis_size(axis))
    route = [(i - distance, i) for i in devices if i - distance in devices]
    return lax.ppermute(block, axis, route)


VMEM_LIMIT = 50 * 1024 * 1024
TAPS = [(a, b) for a in range(3) for b in range(3)]
SPOTS = [(t, i) for t in range(2) for i in range(4)]


def call(body, outs, scratch, place, *operands, after=()):
    vmem = pl.BlockSpec(memory_space=pltpu.VMEM)
    used = 1 + len(operands)
    rest = used + len(after)
    return pl.pallas_call(
        lambda *refs: body(*refs[:used], *refs[rest:]),
        out_shape=outs,
        in_specs=[pl.BlockSpec(memory_space=pltpu.SMEM)]
        + [vmem] * len(operands)
        + [pl.BlockSpec(memory_space=pl.ANY)] * len(after),
        out_specs=[vmem] * len(outs),
        scratch_shapes=scratch,
        compiler_params=pltpu.CompilerParams(vmem_limit_bytes=VMEM_LIMIT),
    )(place, *operands, *after)


def lanes_moved(cell):
    wide = cell.astype(jnp.float32)
    lane = lax.broadcasted_iota(jnp.int32, wide.shape, 1)
    ahead = jnp.where(lane == 127, 0.0, pltpu.roll(wide, 127, 1))
    behind = jnp.where(lane == 0, 0.0, pltpu.roll(wide, 1, 1))
    return ahead.astype(jnp.bfloat16), cell, behind.astype(jnp.bfloat16)


def run_forward(me, own, early, above, below, weight, panel, pre, sent, wide, flat):
    for n in range(9):
        flat[:, n * 256 : n * 256 + 256] = weight[n]
    for f in range(4):
        for r in range(6):
            if r == 0:
                cell = above[f, :256]
            elif r == 5:
                cell = below[f, :256]
            else:
                cell = early[f, r - 1] if f < 2 else own[f - 2, r - 1]
            for k in range(4):
                at = pl.multiple_of(((me + 4 - k) % 4) * 64, 64)
                panel[f * 6 + r, pl.ds(at, 64), :] = cell[k * 64 : k * 64 + 64]
    for p, (t, i) in enumerate(SPOTS):
        for n, (a, b) in enumerate(TAPS):
            wide[n * 256 : n * 256 + 256, p * 128 : p * 128 + 128] = panel[(t + a) * 6 + i + b]
    for t in range(2):
        sums = jnp.dot(
            flat[...], wide[:, t * 512 : t * 512 + 512], preferred_element_type=jnp.float32
        )
        lane = lax.broadcasted_iota(jnp.int32, (64, 128), 1)
        for i in range(4):
            part = sums[:, i * 128 : i * 128 + 128]
            behind = jnp.where(lane == 0, 0.0, pltpu.roll(part[:64], 1, 1))
            ahead = jnp.where(lane == 127, 0.0, pltpu.roll(part[128:], 127, 1))
            value = behind + part[64:128] + ahead
            pre[t * 4 + i] = value
            act = (value * jax.nn.sigmoid(value)).astype(jnp.bfloat16)
            for out in sent:
                out[t * 4 + i] = act


def spread(own, late, above, below, wide, skip=0):
    for f in range(4):
        for r in range(6):
            if r == 0:
                cell = above[f, skip:]
            elif r == 5:
                cell = below[f, skip:]
            else:
                cell = own[f, r - 1] if f < 2 else late[f - 2, r - 1]
            moved = lanes_moved(cell)
            for n, (a, b) in enumerate(TAPS):
                t, i = f - 2 + a, r - 2 + b
                if (t, i) in SPOTS:
                    p = SPOTS.index((t, i))
                    for e in range(3):
                        row = (n * 3 + e) * 64
                        wide[row : row + 64, p * 128 : p * 128 + 128] = moved[e]


def run_transposed(me, weight, wide, full, outs, base):
    full[...] = lax.dot_general(
        weight[...], wide[...], (((0,), (0,)), ((), ())), preferred_element_type=jnp.float32
    )
    for k, out in enumerate(outs):
        at = pl.multiple_of(((me + k) % 4) * 64, 64)
        for p in range(8):
            block = full[pl.ds(at, 64), p * 128 : p * 128 + 128]
            out[p + (base if k else 0)] = block.astype(out.dtype)


def transposed_body(place, own, late, above, below, weight, mine, one, two, three, wide, full):
    spread(own, late, above, below, wide)
    run_transposed(place[0], weight, wide, full, (mine, one, two, three), 0)


def opening_body(
    place, own, early, late, grads, above, below, weight_one, weight_two,
    panel, pre, mine, one, two, three, tall, flat, wide, full,
):
    me = place[0]
    spread(grads, late, above, below, wide, 256)
    run_transposed(me, weight_two, wide, full, (mine, one, two, three), 8)
    run_forward(me, own, early, above, below, weight_one, panel, pre, (one, two, three), tall, flat)


def frame_rows_body(place, early, own, grads, late, heads, tails):
    for f in range(4):
        cells = (early, f) if f < 2 else (own, f - 2)
        others = (grads, f) if f < 2 else (late, f - 2)
        for row, out in ((0, heads), (3, tails)):
            out[f, :256] = cells[0][cells[1], row]
            out[f, 256:] = others[0][others[1], row]


def gradient_rows_body(place, own, late, heads, tails):
    for f in range(4):
        cells = (own, f) if f < 2 else (late, f - 2)
        for row, out in ((0, heads), (3, tails)):
            out[f] = cells[0][cells[1], row]


def against(left, right):
    return lax.dot_general(left, right, (((1,), (1,)), ((), ())), preferred_element_type=jnp.float32)


def store_filter(both, slot, height, tap, rows):
    for q in range(4):
        both[slot, (q + 4 - height) % 4, tap] = rows[q * 16 : q * 16 + 16].astype(jnp.bfloat16)


def filters_body(
    place, panel, pre, mine, r1, r2, r3, sent, own, late, above, below,
    gradient, keep, give, moved, wide, acts, both,
):
    me, height, core = place[0], place[1], place[3]
    for p in range(8):
        value = pre[p]
        sig = jax.nn.sigmoid(value)
        total = mine[p]
        for part in (r1, r2, r3):
            total = total + part[8 + p].astype(jnp.float32)
        total = (total * sig * (1.0 + value * (1.0 - sig))).astype(jnp.bfloat16)
        gradient[p // 4, p % 4] = total
        for e, part in enumerate(lanes_moved(total)):
            moved[e * 64 : e * 64 + 64, p * 128 : p * 128 + 128] = part
    for n, (a, b) in enumerate(TAPS):
        window = jnp.concatenate([panel[(t + a) * 6 + i + b] for t, i in SPOTS], 1)
        sums = against(moved[...], window)
        for e in range(3):
            store_filter(both, core, height, n * 3 + e, sums[e * 64 : e * 64 + 64])
    spread(own, late, above, below, wide, 256)
    for k, part in enumerate((sent, r1, r2, r3)):
        at = pl.multiple_of(((me + 4 - k) % 4) * 64, 64)
        for p in range(8):
            acts[pl.ds(at, 64), p * 128 : p * 128 + 128] = part[p]
    for n in range(9):
        sums = against(wide[n * 192 : n * 192 + 192], acts[...])
        for e in range(3):
            store_filter(both, 1 - core, height, n * 3 + e, sums[e * 64 : e * 64 + 64])
    keep[...] = both[0]
    give[...] = both[1]


def shaped(shape, dtype):
    return jax.ShapeDtypeStruct(shape, dtype)


def opening(place, *operands):
    return call(
        opening_body,
        [shaped((24, 256, 128), jnp.bfloat16)]
        + [shaped((8, 64, 128), jnp.float32)] * 2
        + [shaped((16, 64, 128), jnp.bfloat16)] * 3,
        [
            pltpu.VMEM((2304, 1024), jnp.bfloat16), pltpu.VMEM((192, 2304), jnp.bfloat16),
            pltpu.VMEM((1728, 1024), jnp.bfloat16), pltpu.VMEM((256, 1024), jnp.float32),
        ],
        place, *operands,
    )


def transposed(place, cells, weight):
    return call(
        transposed_body,
        [shaped((8, 64, 128), jnp.float32)] + [shaped((8, 64, 128), jnp.bfloat16)] * 3,
        [pltpu.VMEM((1728, 1024), jnp.bfloat16), pltpu.VMEM((256, 1024), jnp.float32)],
        place, *cells, weight,
    )


def frame_rows(place, *operands):
    return call(frame_rows_body, [shaped((4, 320, 128), jnp.bfloat16)] * 2, [], place, *operands)


def gradient_rows(place, own, late, after):
    rows = [shaped((4, 64, 128), jnp.bfloat16)] * 2
    return call(gradient_rows_body, rows, [], place, own, late, after=after)


def filters(place, *operands):
    return call(
        filters_body,
        [shaped((2, 4, 64, 128), jnp.bfloat16)] + [shaped((4, 27, 16, 256), jnp.bfloat16)] * 2,
        [
            pltpu.VMEM((192, 1024), jnp.bfloat16), pltpu.VMEM((1728, 1024), jnp.bfloat16),
            pltpu.VMEM((256, 1024), jnp.bfloat16), pltpu.VMEM((2, 4, 27, 16, 256), jnp.bfloat16),
        ],
        place, *operands,
    )


def quarters_body(place, own, one, two, three, mine, first, second, third, sums):
    z = place[2]
    total = own[...].astype(jnp.float32)
    for part in (one, two, three):
        total = total + part[...].astype(jnp.float32)
    for q in range(4):
        o, c = (q // 2) * 8, (q % 2) * 128
        sums[q] = total[:, o : o + 8, c : c + 128]
    for k, out in enumerate((mine, first, second, third)):
        out[...] = sums[(z + k) % 4].astype(out.dtype)


def quarters(place, pieces, after):
    small = [shaped((27, 8, 128), jnp.float32)] + [shaped((27, 8, 128), jnp.bfloat16)] * 3
    return call(
        quarters_body, small, [pltpu.VMEM((4, 27, 8, 128), jnp.float32)], place, *pieces, after=after
    )


def rejoined_body(place, own, one, two, three, out, parts):
    z = place[2]
    for k, part in enumerate((own, one, two, three)):
        parts[(z + 4 - k) % 4] = part[...]
    for q in range(4):
        o, c = (q // 2) * 8, (q % 2) * 128
        out[:, o : o + 8, c : c + 128] = parts[q]


def rejoined(place, pieces, after):
    return call(
        rejoined_body, [shaped((27, 16, 256), jnp.bfloat16)],
        [pltpu.VMEM((4, 27, 8, 128), jnp.bfloat16)], place, *pieces, after=after,
    )[0]


def stacked_body(place, own, one, two, three, out):
    height = place[1]
    for k, part in enumerate((own, one, two, three)):
        at = pl.multiple_of(((height + 4 - k) % 4) * 16, 16)
        out[:, pl.ds(at, 16), :] = part[...]


def stacked(place, pieces):
    return call(stacked_body, [shaped((27, 64, 256), jnp.bfloat16)], [], place, *pieces)[0]


def rotated(block, axis, distance):
    count = lax.axis_size(axis)
    return lax.ppermute(block, axis, [(i, (i + distance) % count) for i in range(count)])


def all_rotated(block, axis):
    return [rotated(block, axis, k) for k in range(1, lax.axis_size(axis))]


def sent_on(pieces, axis):
    return [pieces[0]] + [rotated(pieces[k], axis, k) for k in range(1, len(pieces))]


def exchanged(pieces, axis):
    return sum(part.astype(jnp.float32) for part in sent_on(pieces, axis))


def swapped(block, distance):
    return lax.ppermute(block, "tm", [(i, i ^ distance) for i in range(lax.axis_size("tm"))])


def quad_rotated(block, distance):
    route = [(i, i - i % 8 + (i + 2 * distance) % 8) for i in range(lax.axis_size("tm"))]
    return lax.ppermute(block, "tm", route)


def summed_pair(keep, give):
    total = keep.astype(jnp.float32) + swapped(give, 1).astype(jnp.float32)
    return [total[0]] + [total[k].astype(jnp.bfloat16) for k in range(1, 4)]


def rest_of_sum(place, pieces, gradient_pieces, core):
    mine, *others = quarters(place, sent_on(pieces, "height"), [gradient_pieces[0]])
    gradient = exchanged(gradient_pieces, "chan")
    total = mine
    for k, part in enumerate(others):
        total = total + quad_rotated(part, k + 1).astype(jnp.float32)
    total = total.astype(jnp.bfloat16)
    gradient = gradient.reshape(2, 4, 64, 128).astype(jnp.bfloat16)
    total = (total.astype(jnp.float32) + swapped(total, 8).astype(jnp.float32)).astype(jnp.bfloat16)
    total = rejoined(place, [total] + [quad_rotated(total, k) for k in range(1, 4)], [gradient])
    total = stacked(place, [total] + all_rotated(total, "height"))
    other = swapped(total, 1)
    one = jnp.where(core == 1, other, total).astype(jnp.float32)
    two = jnp.where(core == 1, total, other).astype(jnp.float32)
    return gradient, one, two


def filter_shape(flat):
    return flat.reshape(3, 3, 3, 64, 256).transpose(3, 0, 1, 2, 4)


def traded(heads, tails):
    return passed_along(tails, "height", 1), passed_along(heads, "height", -1)


def on_device(frames, grad_out, weight_one, weight_two):
    spot = lax.axis_index("tm")
    core = spot % 2
    place = jnp.stack([lax.axis_index("chan"), lax.axis_index("height"), (spot // 2) % 4, core])
    place = place.astype(jnp.int32)
    taps_one = weight_one.transpose(1, 2, 3, 0, 4).reshape(1728, 256)
    taps_two = weight_two.transpose(1, 2, 3, 0, 4).reshape(1728, 256)
    frames_all = jnp.concatenate([frames] + all_rotated(frames, "chan"), 2)
    early = passed_along(frames_all, "tm", 1)
    late = passed_along(grad_out, "tm", -1)
    above, below = traded(*frame_rows(place, early, frames_all, grad_out, late))
    panel, pre, mine, *sent = opening(
        place, frames_all, early, late, grad_out, above, below, taps_one.reshape(9, 192, 256), taps_two
    )
    received = [rotated(part, "chan", k + 1) for k, part in enumerate(sent)]
    grad_pre, keep, give = filters(
        place, panel, pre, mine, *received, sent[0], grad_out, late, above, below
    )
    pieces = summed_pair(keep, give)
    later = passed_along(grad_pre, "tm", -1)
    edges = traded(*gradient_rows(place, grad_pre, later, [pieces[1]]))
    gradient_pieces = transposed(place, (grad_pre, later) + edges, taps_one)
    grad_frames, grad_one, grad_two = rest_of_sum(place, pieces, gradient_pieces, core)
    return (grad_frames, filter_shape(grad_one), filter_shape(grad_two))


def solution(mesh):
    in_specs = (
        P("tm", "height", "chan", None),
        P("tm", "height", "chan", None),
        P("chan", None, None, None, None),
        P("chan", None, None, None, None),
    )
    out_specs = (
        P("tm", "height", "chan", None),
        P("chan", None, None, None, None),
        P("chan", None, None, None, None),
    )
    return jax.shard_map(
        on_device, mesh=mesh, in_specs=in_specs, out_specs=out_specs, check_vma=False
    )
```

```python
import jax
import jax.numpy as jnp
from jax import lax
from jax.experimental import pallas as pl
from jax.experimental.pallas import tpu as pltpu
from jax.sharding import PartitionSpec as P


def passed_along(block, axis, distance):
    devices = range(lax.axis_size(axis))
    route = [(i - distance, i) for i in devices if i - distance in devices]
    return lax.ppermute(block, axis, route)


VMEM_LIMIT = 50 * 1024 * 1024
TAPS = [(a, b) for a in range(3) for b in range(3)]
SPOTS = [(t, i) for t in range(2) for i in range(4)]


def call(body, outs, scratch, place, *operands, after=()):
    vmem = pl.BlockSpec(memory_space=pltpu.VMEM)
    used = 1 + len(operands)
    rest = used + len(after)
    return pl.pallas_call(
        lambda *refs: body(*refs[:used], *refs[rest:]),
        out_shape=outs,
        in_specs=[pl.BlockSpec(memory_space=pltpu.SMEM)]
        + [vmem] * len(operands)
        + [pl.BlockSpec(memory_space=pl.ANY)] * len(after),
        out_specs=[vmem] * len(outs),
        scratch_shapes=scratch,
        compiler_params=pltpu.CompilerParams(vmem_limit_bytes=VMEM_LIMIT),
    )(place, *operands, *after)


def lanes_moved(cell):
    wide = cell.astype(jnp.float32)
    lane = lax.broadcasted_iota(jnp.int32, wide.shape, 1)
    ahead = jnp.where(lane == 127, 0.0, pltpu.roll(wide, 127, 1))
    behind = jnp.where(lane == 0, 0.0, pltpu.roll(wide, 1, 1))
    return ahead.astype(jnp.bfloat16), cell, behind.astype(jnp.bfloat16)


def run_forward(me, blocks, earlier, weight, panel, pre, sent, wide, flat):
    for n in range(9):
        flat[:, n * 256 : n * 256 + 256] = weight[n]
    for f in range(4):
        for r in range(6):
            for k in range(4):
                at = pl.multiple_of(((me + 4 - k) % 4) * 64, 64)
                cell = earlier[k][f, r] if f < 2 else blocks[k][f - 2, r]
                panel[f * 6 + r, pl.ds(at, 64), :] = cell
    for p, (t, i) in enumerate(SPOTS):
        for n, (a, b) in enumerate(TAPS):
            wide[n * 256 : n * 256 + 256, p * 128 : p * 128 + 128] = panel[(t + a) * 6 + i + b]
    for t in range(2):
        sums = jnp.dot(
            flat[...], wide[:, t * 512 : t * 512 + 512], preferred_element_type=jnp.float32
        )
        lane = lax.broadcasted_iota(jnp.int32, (64, 128), 1)
        for i in range(4):
            part = sums[:, i * 128 : i * 128 + 128]
            behind = jnp.where(lane == 0, 0.0, pltpu.roll(part[:64], 1, 1))
            ahead = jnp.where(lane == 127, 0.0, pltpu.roll(part[128:], 127, 1))
            value = behind + part[64:128] + ahead
            pre[t * 4 + i] = value
            act = (value * jax.nn.sigmoid(value)).astype(jnp.bfloat16)
            for out in sent:
                out[t * 4 + i] = act


def spread(own, late, wide):
    for f in range(4):
        for r in range(6):
            cell = own[f, r] if f < 2 else late[f - 2, r]
            moved = lanes_moved(cell)
            for n, (a, b) in enumerate(TAPS):
                t, i = f - 2 + a, r - 2 + b
                if (t, i) in SPOTS:
                    p = SPOTS.index((t, i))
                    for e in range(3):
                        row = (n * 3 + e) * 64
                        wide[row : row + 64, p * 128 : p * 128 + 128] = moved[e]


def run_transposed(me, weight, wide, full, outs, base):
    full[...] = lax.dot_general(
        weight[...], wide[...], (((0,), (0,)), ((), ())), preferred_element_type=jnp.float32
    )
    for k, out in enumerate(outs):
        at = pl.multiple_of(((me + k) % 4) * 64, 64)
        for p in range(8):
            block = full[pl.ds(at, 64), p * 128 : p * 128 + 128]
            out[p + (base if k else 0)] = block.astype(out.dtype)


def transposed_body(place, own, late, weight, mine, one, two, three, wide, full):
    spread(own, late, wide)
    run_transposed(place[0], weight, wide, full, (mine, one, two, three), 0)


def opening_body(
    place, b0, b1, b2, b3, e0, e1, e2, e3, grads, late, weight_one, weight_two,
    panel, pre, mine, one, two, three, tall, flat, wide, full,
):
    me = place[0]
    spread(grads, late, wide)
    run_transposed(me, weight_two, wide, full, (mine, one, two, three), 8)
    blocks, earlier = (b0, b1, b2, b3), (e0, e1, e2, e3)
    run_forward(me, blocks, earlier, weight_one, panel, pre, (one, two, three), tall, flat)


def outer_rows_body(place, frames, grads, heads, tails):
    for f in range(2):
        for row, out in ((0, heads), (3, tails)):
            out[f] = frames[f, row]
            out[2 + f] = grads[f, row]


def framed_body(place, above, below, *blocks):
    half = len(blocks) // 2
    for n in range(half):
        for f in range(2):
            blocks[half + n][f, 0] = above[2 * n + f]
            blocks[half + n][f, 5] = below[2 * n + f]
            for r in range(4):
                blocks[half + n][f, r + 1] = blocks[n][f, r]


def against(left, right):
    return lax.dot_general(left, right, (((1,), (1,)), ((), ())), preferred_element_type=jnp.float32)


def store_filter(both, slot, height, tap, rows):
    for q in range(4):
        both[slot, (q + 4 - height) % 4, tap] = rows[q * 16 : q * 16 + 16].astype(jnp.bfloat16)


def filters_body(
    place, panel, pre, mine, r1, r2, r3, sent, own, late,
    gradient, heads, tails, keep, give, moved, wide, acts, both,
):
    me, height, core = place[0], place[1], place[3]
    for p in range(8):
        value = pre[p]
        sig = jax.nn.sigmoid(value)
        total = mine[p]
        for part in (r1, r2, r3):
            total = total + part[8 + p].astype(jnp.float32)
        total = (total * sig * (1.0 + value * (1.0 - sig))).astype(jnp.bfloat16)
        gradient[p // 4, p % 4] = total
        if p % 4 == 0:
            heads[p // 4] = total
        if p % 4 == 3:
            tails[p // 4] = total
        for e, part in enumerate(lanes_moved(total)):
            moved[e * 64 : e * 64 + 64, p * 128 : p * 128 + 128] = part
    for n, (a, b) in enumerate(TAPS):
        window = jnp.concatenate([panel[(t + a) * 6 + i + b] for t, i in SPOTS], 1)
        sums = against(moved[...], window)
        for e in range(3):
            store_filter(both, core, height, n * 3 + e, sums[e * 64 : e * 64 + 64])
    spread(own, late, wide)
    for k, part in enumerate((sent, r1, r2, r3)):
        at = pl.multiple_of(((me + 4 - k) % 4) * 64, 64)
        for p in range(8):
            acts[pl.ds(at, 64), p * 128 : p * 128 + 128] = part[p]
    for n in range(9):
        sums = against(wide[n * 192 : n * 192 + 192], acts[...])
        for e in range(3):
            store_filter(both, 1 - core, height, n * 3 + e, sums[e * 64 : e * 64 + 64])
    keep[...] = both[0]
    give[...] = both[1]


def shaped(shape, dtype):
    return jax.ShapeDtypeStruct(shape, dtype)


def opening(place, *operands):
    return call(
        opening_body,
        [shaped((24, 256, 128), jnp.bfloat16)]
        + [shaped((8, 64, 128), jnp.float32)] * 2
        + [shaped((16, 64, 128), jnp.bfloat16)] * 3,
        [
            pltpu.VMEM((2304, 1024), jnp.bfloat16), pltpu.VMEM((192, 2304), jnp.bfloat16),
            pltpu.VMEM((1728, 1024), jnp.bfloat16), pltpu.VMEM((256, 1024), jnp.float32),
        ],
        place, *operands,
    )


def transposed(place, cells, weight):
    return call(
        transposed_body,
        [shaped((8, 64, 128), jnp.float32)] + [shaped((8, 64, 128), jnp.bfloat16)] * 3,
        [pltpu.VMEM((1728, 1024), jnp.bfloat16), pltpu.VMEM((256, 1024), jnp.float32)],
        place, *cells, weight,
    )


def outer_rows(place, frames, grads):
    return call(outer_rows_body, [shaped((4, 64, 128), jnp.bfloat16)] * 2, [], place, frames, grads)


def framed(place, above, below, *blocks, after=()):
    outs = [shaped((2, 6, 64, 128), jnp.bfloat16)] * len(blocks)
    return call(framed_body, outs, [], place, above, below, *blocks, after=after)


def filters(place, *operands):
    return call(
        filters_body,
        [shaped((2, 4, 64, 128), jnp.bfloat16)]
        + [shaped((2, 64, 128), jnp.bfloat16)] * 2
        + [shaped((4, 27, 16, 256), jnp.bfloat16)] * 2,
        [
            pltpu.VMEM((192, 1024), jnp.bfloat16), pltpu.VMEM((1728, 1024), jnp.bfloat16),
            pltpu.VMEM((256, 1024), jnp.bfloat16), pltpu.VMEM((2, 4, 27, 16, 256), jnp.bfloat16),
        ],
        place, *operands,
    )


def quarters_body(place, own, one, two, three, mine, first, second, third, sums):
    z = place[2]
    total = own[...].astype(jnp.float32)
    for part in (one, two, three):
        total = total + part[...].astype(jnp.float32)
    for q in range(4):
        o, c = (q // 2) * 8, (q % 2) * 128
        sums[q] = total[:, o : o + 8, c : c + 128]
    for k, out in enumerate((mine, first, second, third)):
        out[...] = sums[(z + k) % 4].astype(out.dtype)


def quarters(place, pieces, after):
    small = [shaped((27, 8, 128), jnp.float32)] + [shaped((27, 8, 128), jnp.bfloat16)] * 3
    return call(
        quarters_body, small, [pltpu.VMEM((4, 27, 8, 128), jnp.float32)], place, *pieces, after=after
    )


def rejoined_body(place, own, one, two, three, out, parts):
    z = place[2]
    for k, part in enumerate((own, one, two, three)):
        parts[(z + 4 - k) % 4] = part[...]
    for q in range(4):
        o, c = (q // 2) * 8, (q % 2) * 128
        out[:, o : o + 8, c : c + 128] = parts[q]


def rejoined(place, pieces, after):
    return call(
        rejoined_body, [shaped((27, 16, 256), jnp.bfloat16)],
        [pltpu.VMEM((4, 27, 8, 128), jnp.bfloat16)], place, *pieces, after=after,
    )[0]


def stacked_body(place, own, one, two, three, out):
    height = place[1]
    for k, part in enumerate((own, one, two, three)):
        at = pl.multiple_of(((height + 4 - k) % 4) * 16, 16)
        out[:, pl.ds(at, 16), :] = part[...]


def stacked(place, pieces):
    return call(stacked_body, [shaped((27, 64, 256), jnp.bfloat16)], [], place, *pieces)[0]


def rotated(block, axis, distance):
    count = lax.axis_size(axis)
    return lax.ppermute(block, axis, [(i, (i + distance) % count) for i in range(count)])


def all_rotated(block, axis):
    return [rotated(block, axis, k) for k in range(1, lax.axis_size(axis))]


def sent_on(pieces, axis):
    return [pieces[0]] + [rotated(pieces[k], axis, k) for k in range(1, len(pieces))]


def exchanged(pieces, axis):
    return sum(part.astype(jnp.float32) for part in sent_on(pieces, axis))


def swapped(block, distance):
    return lax.ppermute(block, "tm", [(i, i ^ distance) for i in range(lax.axis_size("tm"))])


def quad_rotated(block, distance):
    route = [(i, i - i % 8 + (i + 2 * distance) % 8) for i in range(lax.axis_size("tm"))]
    return lax.ppermute(block, "tm", route)


def summed_pair(keep, give):
    total = keep.astype(jnp.float32) + swapped(give, 1).astype(jnp.float32)
    return [total[0]] + [total[k].astype(jnp.bfloat16) for k in range(1, 4)]


def rest_of_sum(place, pieces, gradient_pieces, core):
    mine, *others = quarters(place, sent_on(pieces, "height"), [gradient_pieces[0]])
    gradient = exchanged(gradient_pieces, "chan")
    total = mine
    for k, part in enumerate(others):
        total = total + quad_rotated(part, k + 1).astype(jnp.float32)
    total = total.astype(jnp.bfloat16)
    gradient = gradient.reshape(2, 4, 64, 128).astype(jnp.bfloat16)
    total = (total.astype(jnp.float32) + swapped(total, 8).astype(jnp.float32)).astype(jnp.bfloat16)
    total = rejoined(place, [total] + [quad_rotated(total, k) for k in range(1, 4)], [gradient])
    total = stacked(place, [total] + all_rotated(total, "height"))
    other = swapped(total, 1)
    one = jnp.where(core == 1, other, total).astype(jnp.float32)
    two = jnp.where(core == 1, total, other).astype(jnp.float32)
    return gradient, one, two


def filter_shape(flat):
    return flat.reshape(3, 3, 3, 64, 256).transpose(3, 0, 1, 2, 4)


def traded(heads, tails):
    return passed_along(tails, "height", 1), passed_along(heads, "height", -1)


def on_device(frames, grad_out, weight_one, weight_two):
    spot = lax.axis_index("tm")
    core = spot % 2
    place = jnp.stack([lax.axis_index("chan"), lax.axis_index("height"), (spot // 2) % 4, core])
    place = place.astype(jnp.int32)
    taps_one = weight_one.transpose(1, 2, 3, 0, 4).reshape(1728, 256)
    taps_two = weight_two.transpose(1, 2, 3, 0, 4).reshape(1728, 256)
    above, below = traded(*outer_rows(place, frames, grad_out))
    block, grads = framed(place, above, below, frames, grad_out)
    early = passed_along(block, "tm", 1)
    late = passed_along(grads, "tm", -1)
    blocks = [block] + all_rotated(block, "chan")
    earlier = [early] + all_rotated(early, "chan")
    panel, pre, mine, *sent = opening(
        place, *blocks, *earlier, grads, late, taps_one.reshape(9, 192, 256), taps_two
    )
    received = [rotated(part, "chan", k + 1) for k, part in enumerate(sent)]
    grad_pre, heads, tails, keep, give = filters(
        place, panel, pre, mine, *received, sent[0], grads, late
    )
    pieces = summed_pair(keep, give)
    above, below = traded(heads, tails)
    cells = framed(place, above, below, grad_pre, after=[pieces[1]])[0]
    later = passed_along(cells, "tm", -1)
    gradient_pieces = transposed(place, (cells, later), taps_one)
    grad_frames, grad_one, grad_two = rest_of_sum(place, pieces, gradient_pieces, core)
    return (grad_frames, filter_shape(grad_one), filter_shape(grad_two))


def solution(mesh):
    in_specs = (
        P("tm", "height", "chan", None),
        P("tm", "height", "chan", None),
        P("chan", None, None, None, None),
        P("chan", None, None, None, None),
    )
    out_specs = (
        P("tm", "height", "chan", None),
        P("chan", None, None, None, None),
        P("chan", None, None, None, None),
    )
    return jax.shard_map(
        on_device, mesh=mesh, in_specs=in_specs, out_specs=out_specs, check_vma=False
    )
```

```python
import jax
import jax.numpy as jnp
from jax import lax
from jax.experimental import pallas as pl
from jax.experimental.pallas import tpu as pltpu
from jax.sharding import PartitionSpec as P


def passed_along(block, axis, distance):
    devices = range(lax.axis_size(axis))
    route = [(i - distance, i) for i in devices if i - distance in devices]
    return lax.ppermute(block, axis, route)


VMEM_LIMIT = 50 * 1024 * 1024
TAPS = [(a, b) for a in range(3) for b in range(3)]
SPOTS = [(t, i) for t in range(2) for i in range(4)]


def call(body, outs, scratch, place, *operands, after=()):
    vmem = pl.BlockSpec(memory_space=pltpu.VMEM)
    used = 1 + len(operands)
    rest = used + len(after)
    return pl.pallas_call(
        lambda *refs: body(*refs[:used], *refs[rest:]),
        out_shape=outs,
        in_specs=[pl.BlockSpec(memory_space=pltpu.SMEM)]
        + [vmem] * len(operands)
        + [pl.BlockSpec(memory_space=pl.ANY)] * len(after),
        out_specs=[vmem] * len(outs),
        scratch_shapes=scratch,
        compiler_params=pltpu.CompilerParams(vmem_limit_bytes=VMEM_LIMIT),
    )(place, *operands, *after)


def lanes_moved(cell):
    wide = cell.astype(jnp.float32)
    lane = lax.broadcasted_iota(jnp.int32, wide.shape, 1)
    ahead = jnp.where(lane == 127, 0.0, pltpu.roll(wide, 127, 1))
    behind = jnp.where(lane == 0, 0.0, pltpu.roll(wide, 1, 1))
    return ahead.astype(jnp.bfloat16), cell, behind.astype(jnp.bfloat16)


def forward_body(place, own, early, above, below, weight, panel, pre, act, wide, flat):
    me = place[0]
    for n in range(9):
        flat[:, n * 256 : n * 256 + 256] = weight[n]
    for f in range(4):
        for r in range(6):
            if r == 0:
                cell = above[f]
            elif r == 5:
                cell = below[f]
            else:
                cell = early[f, r - 1] if f < 2 else own[f - 2, r - 1]
            for k in range(4):
                at = pl.multiple_of(((me + 4 - k) % 4) * 64, 64)
                panel[f * 6 + r, pl.ds(at, 64), :] = cell[k * 64 : k * 64 + 64]
    for p, (t, i) in enumerate(SPOTS):
        for n, (a, b) in enumerate(TAPS):
            wide[n * 256 : n * 256 + 256, p * 128 : p * 128 + 128] = panel[(t + a) * 6 + i + b]
    for t in range(2):
        sums = jnp.dot(
            flat[...], wide[:, t * 512 : t * 512 + 512], preferred_element_type=jnp.float32
        )
        lane = lax.broadcasted_iota(jnp.int32, (64, 128), 1)
        for i in range(4):
            part = sums[:, i * 128 : i * 128 + 128]
            behind = jnp.where(lane == 0, 0.0, pltpu.roll(part[:64], 1, 1))
            ahead = jnp.where(lane == 127, 0.0, pltpu.roll(part[128:], 127, 1))
            value = behind + part[64:128] + ahead
            pre[t * 4 + i] = value
            act[t * 4 + i] = (value * jax.nn.sigmoid(value)).astype(jnp.bfloat16)


def spread(own, late, wide):
    for f in range(4):
        for r in range(6):
            cell = own[f, r] if f < 2 else late[f - 2, r]
            moved = lanes_moved(cell)
            for n, (a, b) in enumerate(TAPS):
                t, i = f - 2 + a, r - 2 + b
                if (t, i) in SPOTS:
                    p = SPOTS.index((t, i))
                    for e in range(3):
                        row = (n * 3 + e) * 64
                        wide[row : row + 64, p * 128 : p * 128 + 128] = moved[e]


def transposed_body(place, own, late, weight, mine, one, two, three, wide, full):
    me = place[0]
    spread(own, late, wide)
    full[...] = lax.dot_general(
        weight[...], wide[...], (((0,), (0,)), ((), ())), preferred_element_type=jnp.float32
    )
    for k, out in enumerate((mine, one, two, three)):
        at = pl.multiple_of(((me + k) % 4) * 64, 64)
        for p in range(8):
            out[p] = full[pl.ds(at, 64), p * 128 : p * 128 + 128].astype(out.dtype)


def frame_rows_body(place, early, own, heads, tails):
    for f in range(4):
        for row, out in ((0, heads), (3, tails)):
            out[f] = early[f, row] if f < 2 else own[f - 2, row]


def edge_rows_body(place, cells, heads, tails):
    for f in range(2):
        heads[f] = cells[f, 0]
        tails[f] = cells[f, 3]


def framed_body(place, above, below, *blocks):
    half = len(blocks) // 2
    for n in range(half):
        for f in range(2):
            blocks[half + n][f, 0] = above[2 * n + f]
            blocks[half + n][f, 5] = below[2 * n + f]
            for r in range(4):
                blocks[half + n][f, r + 1] = blocks[n][f, r]


def against(left, right):
    return lax.dot_general(left, right, (((1,), (1,)), ((), ())), preferred_element_type=jnp.float32)


def store_filter(out, height, tap, rows):
    for q in range(4):
        out[(q + 4 - height) % 4, tap] = rows[q * 16 : q * 16 + 16].astype(jnp.bfloat16)


def first_filter_body(
    place, panel, pre, mine, r1, r2, r3, gradient, heads, tails, result, moved
):
    height = place[1]
    for p in range(8):
        value = pre[p]
        sig = jax.nn.sigmoid(value)
        total = mine[p]
        for part in (r1, r2, r3):
            total = total + part[p].astype(jnp.float32)
        total = (total * sig * (1.0 + value * (1.0 - sig))).astype(jnp.bfloat16)
        gradient[p // 4, p % 4] = total
        if p % 4 == 0:
            heads[p // 4] = total
        if p % 4 == 3:
            tails[p // 4] = total
        for e, part in enumerate(lanes_moved(total)):
            moved[e * 64 : e * 64 + 64, p * 128 : p * 128 + 128] = part
    for n, (a, b) in enumerate(TAPS):
        window = jnp.concatenate([panel[(t + a) * 6 + i + b] for t, i in SPOTS], 1)
        sums = against(moved[...], window)
        for e in range(3):
            store_filter(result, height, n * 3 + e, sums[e * 64 : e * 64 + 64])


def second_filter_body(
    place, first, a0, a1, a2, a3, own, late, keep, give, wide, acts, result
):
    me, height, core = place[0], place[1], place[3]
    spread(own, late, wide)
    for k, part in enumerate((a0, a1, a2, a3)):
        at = pl.multiple_of(((me + 4 - k) % 4) * 64, 64)
        for p in range(8):
            acts[pl.ds(at, 64), p * 128 : p * 128 + 128] = part[p]
    for n in range(9):
        sums = against(wide[n * 192 : n * 192 + 192], acts[...])
        for e in range(3):
            store_filter(result, height, n * 3 + e, sums[e * 64 : e * 64 + 64])

    @pl.when(core == 0)
    def _():
        keep[...] = first[...]
        give[...] = result[...]

    @pl.when(core == 1)
    def _():
        keep[...] = result[...]
        give[...] = first[...]


def shaped(shape, dtype):
    return jax.ShapeDtypeStruct(shape, dtype)


def forward(place, *operands, after):
    return call(
        forward_body,
        [shaped((24, 256, 128), jnp.bfloat16), shaped((8, 64, 128), jnp.float32), shaped((8, 64, 128), jnp.bfloat16)],
        [pltpu.VMEM((2304, 1024), jnp.bfloat16), pltpu.VMEM((192, 2304), jnp.bfloat16)],
        place, *operands, after=after,
    )


def transposed(place, own, late, weight, after=()):
    return call(
        transposed_body,
        [shaped((8, 64, 128), jnp.float32)] + [shaped((8, 64, 128), jnp.bfloat16)] * 3,
        [pltpu.VMEM((1728, 1024), jnp.bfloat16), pltpu.VMEM((256, 1024), jnp.float32)],
        place, own, late, weight, after=after,
    )


def frame_rows(place, early, own):
    return call(frame_rows_body, [shaped((4, 256, 128), jnp.bfloat16)] * 2, [], place, early, own)


def edge_rows(place, cells):
    return call(edge_rows_body, [shaped((2, 64, 128), jnp.bfloat16)] * 2, [], place, cells)


def framed(place, above, below, block):
    out = [shaped((2, 6, 64, 128), jnp.bfloat16)]
    return call(framed_body, out, [], place, above, below, block)[0]


def first_filter(place, *operands):
    return call(
        first_filter_body,
        [shaped((2, 4, 64, 128), jnp.bfloat16)]
        + [shaped((2, 64, 128), jnp.bfloat16)] * 2
        + [shaped((4, 27, 16, 256), jnp.bfloat16)],
        [pltpu.VMEM((192, 1024), jnp.bfloat16)], place, *operands,
    )


def second_filter(place, *operands, after):
    return call(
        second_filter_body,
        [shaped((4, 27, 16, 256), jnp.bfloat16)] * 2,
        [
            pltpu.VMEM((1728, 1024), jnp.bfloat16), pltpu.VMEM((256, 1024), jnp.bfloat16),
            pltpu.VMEM((4, 27, 16, 256), jnp.bfloat16),
        ],
        place, *operands, after=after,
    )


def quarters_body(place, own, one, two, three, mine, first, second, third, sums):
    z = place[2]
    total = own[...].astype(jnp.float32)
    for part in (one, two, three):
        total = total + part[...].astype(jnp.float32)
    for q in range(4):
        o, c = (q // 2) * 8, (q % 2) * 128
        sums[q] = total[:, o : o + 8, c : c + 128]
    for k, out in enumerate((mine, first, second, third)):
        out[...] = sums[(z + k) % 4].astype(out.dtype)


def quarters(place, pieces, after):
    small = [shaped((27, 8, 128), jnp.float32)] + [shaped((27, 8, 128), jnp.bfloat16)] * 3
    return call(
        quarters_body, small, [pltpu.VMEM((4, 27, 8, 128), jnp.float32)], place, *pieces, after=after
    )


def rejoined_body(place, own, one, two, three, out, parts):
    z = place[2]
    for k, part in enumerate((own, one, two, three)):
        parts[(z + 4 - k) % 4] = part[...]
    for q in range(4):
        o, c = (q // 2) * 8, (q % 2) * 128
        out[:, o : o + 8, c : c + 128] = parts[q]


def rejoined(place, pieces, after):
    return call(
        rejoined_body, [shaped((27, 16, 256), jnp.bfloat16)],
        [pltpu.VMEM((4, 27, 8, 128), jnp.bfloat16)], place, *pieces, after=after,
    )[0]


def stacked_body(place, own, one, two, three, out):
    height = place[1]
    for k, part in enumerate((own, one, two, three)):
        at = pl.multiple_of(((height + 4 - k) % 4) * 16, 16)
        out[:, pl.ds(at, 16), :] = part[...]


def stacked(place, pieces):
    return call(stacked_body, [shaped((27, 64, 256), jnp.bfloat16)], [], place, *pieces)[0]


def rotated(block, axis, distance):
    count = lax.axis_size(axis)
    return lax.ppermute(block, axis, [(i, (i + distance) % count) for i in range(count)])


def all_rotated(block, axis):
    return [rotated(block, axis, k) for k in range(1, lax.axis_size(axis))]


def sent_on(pieces, axis):
    return [pieces[0]] + [rotated(pieces[k], axis, k) for k in range(1, len(pieces))]


def exchanged(pieces, axis):
    return sum(part.astype(jnp.float32) for part in sent_on(pieces, axis))


def swapped(block, distance):
    return lax.ppermute(block, "tm", [(i, i ^ distance) for i in range(lax.axis_size("tm"))])


def quad_rotated(block, distance):
    route = [(i, i - i % 8 + (i + 2 * distance) % 8) for i in range(lax.axis_size("tm"))]
    return lax.ppermute(block, "tm", route)


def summed_pair(keep, give):
    total = keep.astype(jnp.float32) + swapped(give, 1).astype(jnp.float32)
    return [total[0]] + [total[k].astype(jnp.bfloat16) for k in range(1, 4)]


def rest_of_sum(place, pieces, gradient_pieces, core):
    mine, *others = quarters(place, sent_on(pieces, "height"), [gradient_pieces[0]])
    gradient = exchanged(gradient_pieces, "chan")
    total = mine
    for k, part in enumerate(others):
        total = total + quad_rotated(part, k + 1).astype(jnp.float32)
    total = total.astype(jnp.bfloat16)
    gradient = gradient.reshape(2, 4, 64, 128).astype(jnp.bfloat16)
    total = (total.astype(jnp.float32) + swapped(total, 8).astype(jnp.float32)).astype(jnp.bfloat16)
    total = rejoined(place, [total] + [quad_rotated(total, k) for k in range(1, 4)], [gradient])
    total = stacked(place, [total] + all_rotated(total, "height"))
    other = swapped(total, 1)
    one = jnp.where(core == 1, other, total).astype(jnp.float32)
    two = jnp.where(core == 1, total, other).astype(jnp.float32)
    return gradient, one, two


def filter_shape(flat):
    return flat.reshape(3, 3, 3, 64, 256).transpose(3, 0, 1, 2, 4)


def traded(heads, tails):
    return passed_along(tails, "height", 1), passed_along(heads, "height", -1)


def on_device(frames, grad_out, weight_one, weight_two):
    spot = lax.axis_index("tm")
    core = spot % 2
    place = jnp.stack([lax.axis_index("chan"), lax.axis_index("height"), (spot // 2) % 4, core])
    place = place.astype(jnp.int32)
    taps_one = weight_one.transpose(1, 2, 3, 0, 4).reshape(1728, 256)
    taps_two = weight_two.transpose(1, 2, 3, 0, 4).reshape(1728, 256)
    frames_all = jnp.concatenate([frames] + all_rotated(frames, "chan"), 2)
    grads = framed(place, *traded(*edge_rows(place, grad_out)), grad_out)
    late = passed_along(grads, "tm", -1)
    early = passed_along(frames_all, "tm", 1)
    above, below = traded(*frame_rows(place, early, frames_all))
    act_pieces = transposed(place, grads, late, taps_two)
    panel, pre, act = forward(
        place, frames_all, early, above, below, taps_one.reshape(9, 192, 256), after=[act_pieces[0]]
    )
    grad_pre, heads, tails, first = first_filter(place, panel, pre, *sent_on(act_pieces, "chan"))
    cells = framed(place, *traded(heads, tails), grad_pre)
    later = passed_along(cells, "tm", -1)
    acts = [act] + all_rotated(act, "chan")
    keep, give = second_filter(place, first, *acts, grads, late, after=[cells])
    pieces = summed_pair(keep, give)
    gradient_pieces = transposed(place, cells, later, taps_one, after=[pieces[1]])
    grad_frames, grad_one, grad_two = rest_of_sum(place, pieces, gradient_pieces, core)
    return (grad_frames, filter_shape(grad_one), filter_shape(grad_two))


def solution(mesh):
    in_specs = (
        P("tm", "height", "chan", None),
        P("tm", "height", "chan", None),
        P("chan", None, None, None, None),
        P("chan", None, None, None, None),
    )
    out_specs = (
        P("tm", "height", "chan", None),
        P("chan", None, None, None, None),
        P("chan", None, None, None, None),
    )
    return jax.shard_map(
        on_device, mesh=mesh, in_specs=in_specs, out_specs=out_specs, check_vma=False
    )
```

```python
import jax
import jax.numpy as jnp
from jax import lax
from jax.experimental import pallas as pl
from jax.experimental.pallas import tpu as pltpu
from jax.sharding import PartitionSpec as P


def passed_along(block, axis, distance):
    devices = range(lax.axis_size(axis))
    route = [(i - distance, i) for i in devices if i - distance in devices]
    return lax.ppermute(block, axis, route)


VMEM_LIMIT = 24 * 1024 * 1024
TAPS = [(a, b) for a in range(3) for b in range(3)]
SPOTS = [(t, i) for t in range(2) for i in range(4)]


def call(body, outs, scratch, place, *operands, after=()):
    vmem = pl.BlockSpec(memory_space=pltpu.VMEM)
    used = 1 + len(operands)
    rest = used + len(after)
    return pl.pallas_call(
        lambda *refs: body(*refs[:used], *refs[rest:]),
        out_shape=outs,
        in_specs=[pl.BlockSpec(memory_space=pltpu.SMEM)]
        + [vmem] * len(operands)
        + [pl.BlockSpec(memory_space=pl.ANY)] * len(after),
        out_specs=[vmem] * len(outs),
        scratch_shapes=scratch,
        compiler_params=pltpu.CompilerParams(vmem_limit_bytes=VMEM_LIMIT),
    )(place, *operands, *after)


def lanes_moved(cell):
    wide = cell.astype(jnp.float32)
    lane = lax.broadcasted_iota(jnp.int32, wide.shape, 1)
    ahead = jnp.where(lane == 127, 0.0, pltpu.roll(wide, 127, 1))
    behind = jnp.where(lane == 0, 0.0, pltpu.roll(wide, 1, 1))
    return ahead.astype(jnp.bfloat16), cell, behind.astype(jnp.bfloat16)


def forward_body(place, own, early, above, below, weight, panel, pre, act, wide, flat):
    me = place[0]
    for n in range(9):
        flat[:, n * 256 : n * 256 + 256] = weight[n]
    for f in range(4):
        for r in range(6):
            if r == 0:
                cell = above[f]
            elif r == 5:
                cell = below[f]
            else:
                cell = early[f, r - 1] if f < 2 else own[f - 2, r - 1]
            for k in range(4):
                at = pl.multiple_of(((me + 4 - k) % 4) * 64, 64)
                panel[f * 6 + r, pl.ds(at, 64), :] = cell[k * 64 : k * 64 + 64]
    for p, (t, i) in enumerate(SPOTS):
        for n, (a, b) in enumerate(TAPS):
            wide[n * 256 : n * 256 + 256, p * 128 : p * 128 + 128] = panel[(t + a) * 6 + i + b]
    for t in range(2):
        sums = jnp.dot(
            flat[...], wide[:, t * 512 : t * 512 + 512], preferred_element_type=jnp.float32
        )
        lane = lax.broadcasted_iota(jnp.int32, (64, 128), 1)
        for i in range(4):
            part = sums[:, i * 128 : i * 128 + 128]
            behind = jnp.where(lane == 0, 0.0, pltpu.roll(part[:64], 1, 1))
            ahead = jnp.where(lane == 127, 0.0, pltpu.roll(part[128:], 127, 1))
            value = behind + part[64:128] + ahead
            pre[t * 4 + i] = value
            act[t * 4 + i] = (value * jax.nn.sigmoid(value)).astype(jnp.bfloat16)


def spread(own, late, wide):
    for f in range(4):
        for r in range(6):
            cell = own[f, r] if f < 2 else late[f - 2, r]
            moved = lanes_moved(cell)
            for n, (a, b) in enumerate(TAPS):
                t, i = f - 2 + a, r - 2 + b
                if (t, i) in SPOTS:
                    p = SPOTS.index((t, i))
                    for e in range(3):
                        row = (n * 3 + e) * 64
                        wide[row : row + 64, p * 128 : p * 128 + 128] = moved[e]


def transposed_body(place, own, late, weight, mine, one, two, three, wide, full):
    me = place[0]
    spread(own, late, wide)
    full[...] = lax.dot_general(
        weight[...], wide[...], (((0,), (0,)), ((), ())), preferred_element_type=jnp.float32
    )
    for k, out in enumerate((mine, one, two, three)):
        at = pl.multiple_of(((me + k) % 4) * 64, 64)
        for p in range(8):
            out[p] = full[pl.ds(at, 64), p * 128 : p * 128 + 128].astype(out.dtype)


def frame_rows_body(place, early, own, heads, tails):
    for f in range(4):
        for row, out in ((0, heads), (3, tails)):
            out[f] = early[f, row] if f < 2 else own[f - 2, row]


def edge_rows_body(place, cells, heads, tails):
    for f in range(2):
        heads[f] = cells[f, 0]
        tails[f] = cells[f, 3]


def framed_body(place, above, below, *blocks):
    half = len(blocks) // 2
    for n in range(half):
        for f in range(2):
            blocks[half + n][f, 0] = above[2 * n + f]
            blocks[half + n][f, 5] = below[2 * n + f]
            for r in range(4):
                blocks[half + n][f, r + 1] = blocks[n][f, r]


def against(left, right):
    return lax.dot_general(left, right, (((1,), (1,)), ((), ())), preferred_element_type=jnp.float32)


def store_filter(out, height, tap, rows):
    for q in range(4):
        out[(q + 4 - height) % 4, tap] = rows[q * 16 : q * 16 + 16].astype(jnp.bfloat16)


def first_filter_body(
    place, panel, pre, mine, r1, r2, r3, gradient, heads, tails, result, moved
):
    height = place[1]
    for p in range(8):
        value = pre[p]
        sig = jax.nn.sigmoid(value)
        total = mine[p]
        for part in (r1, r2, r3):
            total = total + part[p].astype(jnp.float32)
        total = (total * sig * (1.0 + value * (1.0 - sig))).astype(jnp.bfloat16)
        gradient[p // 4, p % 4] = total
        if p % 4 == 0:
            heads[p // 4] = total
        if p % 4 == 3:
            tails[p // 4] = total
        for e, part in enumerate(lanes_moved(total)):
            moved[e * 64 : e * 64 + 64, p * 128 : p * 128 + 128] = part
    for n, (a, b) in enumerate(TAPS):
        window = jnp.concatenate([panel[(t + a) * 6 + i + b] for t, i in SPOTS], 1)
        sums = against(moved[...], window)
        for e in range(3):
            store_filter(result, height, n * 3 + e, sums[e * 64 : e * 64 + 64])


def second_filter_body(
    place, first, a0, a1, a2, a3, own, late, keep, give, wide, acts, result
):
    me, height, core = place[0], place[1], place[3]
    spread(own, late, wide)
    for k, part in enumerate((a0, a1, a2, a3)):
        at = pl.multiple_of(((me + 4 - k) % 4) * 64, 64)
        for p in range(8):
            acts[pl.ds(at, 64), p * 128 : p * 128 + 128] = part[p]
    for n in range(9):
        sums = against(wide[n * 192 : n * 192 + 192], acts[...])
        for e in range(3):
            store_filter(result, height, n * 3 + e, sums[e * 64 : e * 64 + 64])

    @pl.when(core == 0)
    def _():
        keep[...] = first[...]
        give[...] = result[...]

    @pl.when(core == 1)
    def _():
        keep[...] = result[...]
        give[...] = first[...]


def shaped(shape, dtype):
    return jax.ShapeDtypeStruct(shape, dtype)


def forward(place, *operands, after):
    return call(
        forward_body,
        [shaped((24, 256, 128), jnp.bfloat16), shaped((8, 64, 128), jnp.float32), shaped((8, 64, 128), jnp.bfloat16)],
        [pltpu.VMEM((2304, 1024), jnp.bfloat16), pltpu.VMEM((192, 2304), jnp.bfloat16)],
        place, *operands, after=after,
    )


def transposed(place, own, late, weight, after=()):
    return call(
        transposed_body,
        [shaped((8, 64, 128), jnp.float32)] + [shaped((8, 64, 128), jnp.bfloat16)] * 3,
        [pltpu.VMEM((1728, 1024), jnp.bfloat16), pltpu.VMEM((256, 1024), jnp.float32)],
        place, own, late, weight, after=after,
    )


def frame_rows(place, early, own):
    return call(frame_rows_body, [shaped((4, 256, 128), jnp.bfloat16)] * 2, [], place, early, own)


def edge_rows(place, cells):
    return call(edge_rows_body, [shaped((2, 64, 128), jnp.bfloat16)] * 2, [], place, cells)


def framed(place, above, below, block):
    out = [shaped((2, 6, 64, 128), jnp.bfloat16)]
    return call(framed_body, out, [], place, above, below, block)[0]


def first_filter(place, *operands):
    return call(
        first_filter_body,
        [shaped((2, 4, 64, 128), jnp.bfloat16)]
        + [shaped((2, 64, 128), jnp.bfloat16)] * 2
        + [shaped((4, 27, 16, 256), jnp.bfloat16)],
        [pltpu.VMEM((192, 1024), jnp.bfloat16)], place, *operands,
    )


def second_filter(place, *operands, after):
    return call(
        second_filter_body,
        [shaped((4, 27, 16, 256), jnp.bfloat16)] * 2,
        [
            pltpu.VMEM((1728, 1024), jnp.bfloat16), pltpu.VMEM((256, 1024), jnp.bfloat16),
            pltpu.VMEM((4, 27, 16, 256), jnp.bfloat16),
        ],
        place, *operands, after=after,
    )


def quarters_body(place, own, one, two, three, mine, first, second, third, sums):
    z = place[2]
    total = own[...].astype(jnp.float32)
    for part in (one, two, three):
        total = total + part[...].astype(jnp.float32)
    for q in range(4):
        o, c = (q // 2) * 8, (q % 2) * 128
        sums[q] = total[:, o : o + 8, c : c + 128]
    for k, out in enumerate((mine, first, second, third)):
        out[...] = sums[(z + k) % 4].astype(out.dtype)


def quarters(place, pieces, after):
    small = [shaped((27, 8, 128), jnp.float32)] + [shaped((27, 8, 128), jnp.bfloat16)] * 3
    return call(
        quarters_body, small, [pltpu.VMEM((4, 27, 8, 128), jnp.float32)], place, *pieces, after=after
    )


def rejoined_body(place, own, one, two, three, out, parts):
    z = place[2]
    for k, part in enumerate((own, one, two, three)):
        parts[(z + 4 - k) % 4] = part[...]
    for q in range(4):
        o, c = (q // 2) * 8, (q % 2) * 128
        out[:, o : o + 8, c : c + 128] = parts[q]


def rejoined(place, pieces, after):
    return call(
        rejoined_body, [shaped((27, 16, 256), jnp.bfloat16)],
        [pltpu.VMEM((4, 27, 8, 128), jnp.bfloat16)], place, *pieces, after=after,
    )[0]


def stacked_body(place, own, one, two, three, out):
    height = place[1]
    for k, part in enumerate((own, one, two, three)):
        at = pl.multiple_of(((height + 4 - k) % 4) * 16, 16)
        out[:, pl.ds(at, 16), :] = part[...]


def stacked(place, pieces):
    return call(stacked_body, [shaped((27, 64, 256), jnp.bfloat16)], [], place, *pieces)[0]


def rotated(block, axis, distance):
    count = lax.axis_size(axis)
    return lax.ppermute(block, axis, [(i, (i + distance) % count) for i in range(count)])


def all_rotated(block, axis):
    return [rotated(block, axis, k) for k in range(1, lax.axis_size(axis))]


def sent_on(pieces, axis):
    return [pieces[0]] + [rotated(pieces[k], axis, k) for k in range(1, len(pieces))]


def exchanged(pieces, axis):
    return sum(part.astype(jnp.float32) for part in sent_on(pieces, axis))


def swapped(block, distance):
    return lax.ppermute(block, "tm", [(i, i ^ distance) for i in range(lax.axis_size("tm"))])


def quad_rotated(block, distance):
    route = [(i, i - i % 8 + (i + 2 * distance) % 8) for i in range(lax.axis_size("tm"))]
    return lax.ppermute(block, "tm", route)


def summed_pair(keep, give):
    total = keep.astype(jnp.float32) + swapped(give, 1).astype(jnp.float32)
    return [total[0]] + [total[k].astype(jnp.bfloat16) for k in range(1, 4)]


def rest_of_sum(place, pieces, gradient_pieces, core):
    mine, *others = quarters(place, sent_on(pieces, "height"), [gradient_pieces[0]])
    gradient = exchanged(gradient_pieces, "chan")
    total = mine
    for k, part in enumerate(others):
        total = total + quad_rotated(part, k + 1).astype(jnp.float32)
    total = total.astype(jnp.bfloat16)
    gradient = gradient.reshape(2, 4, 64, 128).astype(jnp.bfloat16)
    total = (total.astype(jnp.float32) + swapped(total, 8).astype(jnp.float32)).astype(jnp.bfloat16)
    total = rejoined(place, [total] + [quad_rotated(total, k) for k in range(1, 4)], [gradient])
    total = stacked(place, [total] + all_rotated(total, "height"))
    other = swapped(total, 1)
    one = jnp.where(core == 1, other, total).astype(jnp.float32)
    two = jnp.where(core == 1, total, other).astype(jnp.float32)
    return gradient, one, two


def filter_shape(flat):
    return flat.reshape(3, 3, 3, 64, 256).transpose(3, 0, 1, 2, 4)


def traded(heads, tails):
    return passed_along(tails, "height", 1), passed_along(heads, "height", -1)


def on_device(frames, grad_out, weight_one, weight_two):
    spot = lax.axis_index("tm")
    core = spot % 2
    place = jnp.stack([lax.axis_index("chan"), lax.axis_index("height"), (spot // 2) % 4, core])
    place = place.astype(jnp.int32)
    taps_one = weight_one.transpose(1, 2, 3, 0, 4).reshape(1728, 256)
    taps_two = weight_two.transpose(1, 2, 3, 0, 4).reshape(1728, 256)
    frames_all = jnp.concatenate([frames] + all_rotated(frames, "chan"), 2)
    grads = framed(place, *traded(*edge_rows(place, grad_out)), grad_out)
    late = passed_along(grads, "tm", -1)
    early = passed_along(frames_all, "tm", 1)
    above, below = traded(*frame_rows(place, early, frames_all))
    act_pieces = transposed(place, grads, late, taps_two)
    panel, pre, act = forward(
        place, frames_all, early, above, below, taps_one.reshape(9, 192, 256), after=[act_pieces[0]]
    )
    grad_pre, heads, tails, first = first_filter(place, panel, pre, *sent_on(act_pieces, "chan"))
    cells = framed(place, *traded(heads, tails), grad_pre)
    later = passed_along(cells, "tm", -1)
    acts = [act] + all_rotated(act, "chan")
    keep, give = second_filter(place, first, *acts, grads, late, after=[cells])
    pieces = summed_pair(keep, give)
    gradient_pieces = transposed(place, cells, later, taps_one, after=[pieces[1]])
    grad_frames, grad_one, grad_two = rest_of_sum(place, pieces, gradient_pieces, core)
    return (grad_frames, filter_shape(grad_one), filter_shape(grad_two))


def solution(mesh):
    in_specs = (
        P("tm", "height", "chan", None),
        P("tm", "height", "chan", None),
        P("chan", None, None, None, None),
        P("chan", None, None, None, None),
    )
    out_specs = (
        P("tm", "height", "chan", None),
        P("chan", None, None, None, None),
        P("chan", None, None, None, None),
    )
    return jax.shard_map(
        on_device, mesh=mesh, in_specs=in_specs, out_specs=out_specs, check_vma=False
    )
```

```python
import jax
import jax.numpy as jnp
from jax import lax
from jax.experimental import pallas as pl
from jax.experimental.pallas import tpu as pltpu
from jax.sharding import PartitionSpec as P


def passed_along(block, axis, distance):
    devices = range(lax.axis_size(axis))
    route = [(i - distance, i) for i in devices if i - distance in devices]
    return lax.ppermute(block, axis, route)


VMEM_LIMIT = 24 * 1024 * 1024
TAPS = [(a, b) for a in range(3) for b in range(3)]
SPOTS = [(t, i) for t in range(2) for i in range(4)]


def call(body, outs, scratch, place, *operands, after=()):
    vmem = pl.BlockSpec(memory_space=pltpu.VMEM)
    used = 1 + len(operands)
    rest = used + len(after)
    return pl.pallas_call(
        lambda *refs: body(*refs[:used], *refs[rest:]),
        out_shape=outs,
        in_specs=[pl.BlockSpec(memory_space=pltpu.SMEM)]
        + [vmem] * len(operands)
        + [pl.BlockSpec(memory_space=pl.ANY)] * len(after),
        out_specs=[vmem] * len(outs),
        scratch_shapes=scratch,
        compiler_params=pltpu.CompilerParams(vmem_limit_bytes=VMEM_LIMIT),
    )(place, *operands, *after)


def lanes_moved(cell):
    wide = cell.astype(jnp.float32)
    lane = lax.broadcasted_iota(jnp.int32, wide.shape, 1)
    ahead = jnp.where(lane == 127, 0.0, pltpu.roll(wide, 127, 1))
    behind = jnp.where(lane == 0, 0.0, pltpu.roll(wide, 1, 1))
    return ahead.astype(jnp.bfloat16), cell, behind.astype(jnp.bfloat16)


def forward_body(place, own, early, above, below, weight, panel, pre, act, wide, flat):
    me = place[0]
    for n in range(9):
        flat[:, n * 256 : n * 256 + 256] = weight[n]
    for f in range(4):
        for r in range(6):
            if r == 0:
                cell = above[f]
            elif r == 5:
                cell = below[f]
            else:
                cell = early[f, r - 1] if f < 2 else own[f - 2, r - 1]
            for k in range(4):
                at = pl.multiple_of(((me + 4 - k) % 4) * 64, 64)
                panel[f * 6 + r, pl.ds(at, 64), :] = cell[k * 64 : k * 64 + 64]
    for p, (t, i) in enumerate(SPOTS):
        for n, (a, b) in enumerate(TAPS):
            wide[n * 256 : n * 256 + 256, p * 128 : p * 128 + 128] = panel[(t + a) * 6 + i + b]
    for t in range(2):
        sums = jnp.dot(
            flat[...], wide[:, t * 512 : t * 512 + 512], preferred_element_type=jnp.float32
        )
        lane = lax.broadcasted_iota(jnp.int32, (64, 128), 1)
        for i in range(4):
            part = sums[:, i * 128 : i * 128 + 128]
            behind = jnp.where(lane == 0, 0.0, pltpu.roll(part[:64], 1, 1))
            ahead = jnp.where(lane == 127, 0.0, pltpu.roll(part[128:], 127, 1))
            value = behind + part[64:128] + ahead
            pre[t * 4 + i] = value
            act[t * 4 + i] = (value * jax.nn.sigmoid(value)).astype(jnp.bfloat16)


def spread(own, late, wide):
    for f in range(4):
        for r in range(6):
            cell = own[f, r] if f < 2 else late[f - 2, r]
            moved = lanes_moved(cell)
            for n, (a, b) in enumerate(TAPS):
                t, i = f - 2 + a, r - 2 + b
                if (t, i) in SPOTS:
                    p = SPOTS.index((t, i))
                    for e in range(3):
                        row = (n * 3 + e) * 64
                        wide[row : row + 64, p * 128 : p * 128 + 128] = moved[e]


def transposed_body(place, own, late, weight, mine, one, two, three, wide, full):
    me = place[0]
    spread(own, late, wide)
    full[...] = lax.dot_general(
        weight[...], wide[...], (((0,), (0,)), ((), ())), preferred_element_type=jnp.float32
    )
    for k, out in enumerate((mine, one, two, three)):
        at = pl.multiple_of(((me + k) % 4) * 64, 64)
        for p in range(8):
            out[p] = full[pl.ds(at, 64), p * 128 : p * 128 + 128].astype(out.dtype)


def frame_rows_body(place, early, own, heads, tails):
    for f in range(4):
        for row, out in ((0, heads), (3, tails)):
            out[f] = early[f, row] if f < 2 else own[f - 2, row]


def edge_rows_body(place, cells, heads, tails):
    for f in range(2):
        heads[f] = cells[f, 0]
        tails[f] = cells[f, 3]


def framed_body(place, above, below, *blocks):
    half = len(blocks) // 2
    for n in range(half):
        for f in range(2):
            blocks[half + n][f, 0] = above[2 * n + f]
            blocks[half + n][f, 5] = below[2 * n + f]
            for r in range(4):
                blocks[half + n][f, r + 1] = blocks[n][f, r]


def against(left, right):
    return lax.dot_general(left, right, (((1,), (1,)), ((), ())), preferred_element_type=jnp.float32)


def store_filter(out, height, tap, rows):
    for q in range(4):
        out[(q + 4 - height) % 4, tap] = rows[q * 16 : q * 16 + 16].astype(jnp.bfloat16)


def first_filter_body(
    place, panel, pre, mine, r1, r2, r3, gradient, heads, tails, result, moved
):
    height = place[1]
    for p in range(8):
        value = pre[p]
        sig = jax.nn.sigmoid(value)
        total = mine[p]
        for part in (r1, r2, r3):
            total = total + part[p].astype(jnp.float32)
        total = (total * sig * (1.0 + value * (1.0 - sig))).astype(jnp.bfloat16)
        gradient[p // 4, p % 4] = total
        if p % 4 == 0:
            heads[p // 4] = total
        if p % 4 == 3:
            tails[p // 4] = total
        for e, part in enumerate(lanes_moved(total)):
            moved[e * 64 : e * 64 + 64, p * 128 : p * 128 + 128] = part
    for n, (a, b) in enumerate(TAPS):
        window = jnp.concatenate([panel[(t + a) * 6 + i + b] for t, i in SPOTS], 1)
        sums = against(moved[...], window)
        for e in range(3):
            store_filter(result, height, n * 3 + e, sums[e * 64 : e * 64 + 64])


def second_filter_body(
    place, first, a0, a1, a2, a3, own, late, keep, give, wide, acts, result
):
    me, height, core = place[0], place[1], place[3]
    spread(own, late, wide)
    for k, part in enumerate((a0, a1, a2, a3)):
        at = pl.multiple_of(((me + 4 - k) % 4) * 64, 64)
        for p in range(8):
            acts[pl.ds(at, 64), p * 128 : p * 128 + 128] = part[p]
    for n in range(9):
        sums = against(wide[n * 192 : n * 192 + 192], acts[...])
        for e in range(3):
            store_filter(result, height, n * 3 + e, sums[e * 64 : e * 64 + 64])

    @pl.when(core == 0)
    def _():
        keep[...] = first[...]
        give[...] = result[...]

    @pl.when(core == 1)
    def _():
        keep[...] = result[...]
        give[...] = first[...]


def shaped(shape, dtype):
    return jax.ShapeDtypeStruct(shape, dtype)


def forward(place, *operands, after):
    return call(
        forward_body,
        [shaped((24, 256, 128), jnp.bfloat16), shaped((8, 64, 128), jnp.float32), shaped((8, 64, 128), jnp.bfloat16)],
        [pltpu.VMEM((2304, 1024), jnp.bfloat16), pltpu.VMEM((192, 2304), jnp.bfloat16)],
        place, *operands, after=after,
    )


def transposed(place, own, late, weight, after=()):
    return call(
        transposed_body,
        [shaped((8, 64, 128), jnp.float32)] + [shaped((8, 64, 128), jnp.bfloat16)] * 3,
        [pltpu.VMEM((1728, 1024), jnp.bfloat16), pltpu.VMEM((256, 1024), jnp.float32)],
        place, own, late, weight, after=after,
    )


def frame_rows(place, early, own):
    return call(frame_rows_body, [shaped((4, 256, 128), jnp.bfloat16)] * 2, [], place, early, own)


def edge_rows(place, cells):
    return call(edge_rows_body, [shaped((2, 64, 128), jnp.bfloat16)] * 2, [], place, cells)


def framed(place, above, below, block):
    out = [shaped((2, 6, 64, 128), jnp.bfloat16)]
    return call(framed_body, out, [], place, above, below, block)[0]


def first_filter(place, *operands):
    return call(
        first_filter_body,
        [shaped((2, 4, 64, 128), jnp.bfloat16)]
        + [shaped((2, 64, 128), jnp.bfloat16)] * 2
        + [shaped((4, 27, 16, 256), jnp.bfloat16)],
        [pltpu.VMEM((192, 1024), jnp.bfloat16)], place, *operands,
    )


def second_filter(place, *operands, after):
    return call(
        second_filter_body,
        [shaped((4, 27, 16, 256), jnp.bfloat16)] * 2,
        [
            pltpu.VMEM((1728, 1024), jnp.bfloat16), pltpu.VMEM((256, 1024), jnp.bfloat16),
            pltpu.VMEM((4, 27, 16, 256), jnp.bfloat16),
        ],
        place, *operands, after=after,
    )


def quarters_body(place, own, one, two, three, mine, first, second, third, sums):
    z = place[2]
    total = own[...].astype(jnp.float32)
    for part in (one, two, three):
        total = total + part[...].astype(jnp.float32)
    for q in range(4):
        o, c = (q // 2) * 8, (q % 2) * 128
        sums[q] = total[:, o : o + 8, c : c + 128]
    for k, out in enumerate((mine, first, second, third)):
        out[...] = sums[(z + k) % 4].astype(out.dtype)


def quarters(place, pieces, after):
    small = [shaped((27, 8, 128), jnp.float32)] + [shaped((27, 8, 128), jnp.bfloat16)] * 3
    return call(
        quarters_body, small, [pltpu.VMEM((4, 27, 8, 128), jnp.float32)], place, *pieces, after=after
    )


def rejoined_body(place, own, one, two, three, out, parts):
    z = place[2]
    for k, part in enumerate((own, one, two, three)):
        parts[(z + 4 - k) % 4] = part[...]
    for q in range(4):
        o, c = (q // 2) * 8, (q % 2) * 128
        out[:, o : o + 8, c : c + 128] = parts[q]


def rejoined(place, pieces, after):
    return call(
        rejoined_body, [shaped((27, 16, 256), jnp.bfloat16)],
        [pltpu.VMEM((4, 27, 8, 128), jnp.bfloat16)], place, *pieces, after=after,
    )[0]


def stacked_body(place, own, one, two, three, out):
    height = place[1]
    for k, part in enumerate((own, one, two, three)):
        at = pl.multiple_of(((height + 4 - k) % 4) * 16, 16)
        out[:, pl.ds(at, 16), :] = part[...]


def stacked(place, pieces, after):
    return call(stacked_body, [shaped((27, 64, 256), jnp.bfloat16)], [], place, *pieces, after=after)[0]


def rotated(block, axis, distance):
    count = lax.axis_size(axis)
    return lax.ppermute(block, axis, [(i, (i + distance) % count) for i in range(count)])


def all_rotated(block, axis):
    return [rotated(block, axis, k) for k in range(1, lax.axis_size(axis))]


def sent_on(pieces, axis):
    return [pieces[0]] + [rotated(pieces[k], axis, k) for k in range(1, len(pieces))]


def exchanged(pieces, axis):
    return sum(part.astype(jnp.float32) for part in sent_on(pieces, axis))


def swapped(block, distance):
    return lax.ppermute(block, "tm", [(i, i ^ distance) for i in range(lax.axis_size("tm"))])


def quad_rotated(block, distance):
    route = [(i, i - i % 8 + (i + 2 * distance) % 8) for i in range(lax.axis_size("tm"))]
    return lax.ppermute(block, "tm", route)


def summed_pair(keep, give):
    total = keep.astype(jnp.float32) + swapped(give, 1).astype(jnp.float32)
    return [total[0]] + [total[k].astype(jnp.bfloat16) for k in range(1, 4)]


def rest_of_sum(place, pieces, gradient_pieces, core):
    mine, *others = quarters(place, sent_on(pieces, "height"), [gradient_pieces[0]])
    gradient = exchanged(gradient_pieces, "chan")
    total = mine
    for k, part in enumerate(others):
        total = total + quad_rotated(part, k + 1).astype(jnp.float32)
    total = total.astype(jnp.bfloat16)
    gradient = gradient.reshape(2, 4, 64, 128).astype(jnp.bfloat16)
    total = (total.astype(jnp.float32) + swapped(total, 8).astype(jnp.float32)).astype(jnp.bfloat16)
    total = rejoined(place, [total] + [quad_rotated(total, k) for k in range(1, 4)], [])
    total = stacked(place, [total] + all_rotated(total, "height"), [gradient])
    other = swapped(total, 1)
    one = jnp.where(core == 1, other, total).astype(jnp.float32)
    two = jnp.where(core == 1, total, other).astype(jnp.float32)
    return gradient, one, two


def filter_shape(flat):
    return flat.reshape(3, 3, 3, 64, 256).transpose(3, 0, 1, 2, 4)


def traded(heads, tails):
    return passed_along(tails, "height", 1), passed_along(heads, "height", -1)


def on_device(frames, grad_out, weight_one, weight_two):
    spot = lax.axis_index("tm")
    core = spot % 2
    place = jnp.stack([lax.axis_index("chan"), lax.axis_index("height"), (spot // 2) % 4, core])
    place = place.astype(jnp.int32)
    taps_one = weight_one.transpose(1, 2, 3, 0, 4).reshape(1728, 256)
    taps_two = weight_two.transpose(1, 2, 3, 0, 4).reshape(1728, 256)
    frames_all = jnp.concatenate([frames] + all_rotated(frames, "chan"), 2)
    grads = framed(place, *traded(*edge_rows(place, grad_out)), grad_out)
    late = passed_along(grads, "tm", -1)
    early = passed_along(frames_all, "tm", 1)
    above, below = traded(*frame_rows(place, early, frames_all))
    act_pieces = transposed(place, grads, late, taps_two)
    panel, pre, act = forward(
        place, frames_all, early, above, below, taps_one.reshape(9, 192, 256), after=[act_pieces[0]]
    )
    grad_pre, heads, tails, first = first_filter(place, panel, pre, *sent_on(act_pieces, "chan"))
    cells = framed(place, *traded(heads, tails), grad_pre)
    later = passed_along(cells, "tm", -1)
    acts = [act] + all_rotated(act, "chan")
    keep, give = second_filter(place, first, *acts, grads, late, after=[cells])
    pieces = summed_pair(keep, give)
    gradient_pieces = transposed(place, cells, later, taps_one, after=[pieces[1]])
    grad_frames, grad_one, grad_two = rest_of_sum(place, pieces, gradient_pieces, core)
    return (grad_frames, filter_shape(grad_one), filter_shape(grad_two))


def solution(mesh):
    in_specs = (
        P("tm", "height", "chan", None),
        P("tm", "height", "chan", None),
        P("chan", None, None, None, None),
        P("chan", None, None, None, None),
    )
    out_specs = (
        P("tm", "height", "chan", None),
        P("chan", None, None, None, None),
        P("chan", None, None, None, None),
    )
    return jax.shard_map(
        on_device, mesh=mesh, in_specs=in_specs, out_specs=out_specs, check_vma=False
    )
```
